256 devices in a mesh: section: 2 (over y_hi), seq: 32 (over x, z), tensor: 4 (over y_lo, core).
Axes of the slice: x: 4, y: 4 (y_hi: 2, y_lo: 2; y = y_hi * 2 + y_lo), z: 8, core: 2. Of those that a mesh axis runs over, the one named last changes fastest.
Arguments:
- q_mant: bfloat16 [2, 2048, 16384], P('section', 'seq', 'tensor'), may hold values from -32 to 32
- q_scale: int32 [2, 2048, 512], P('section', 'seq', 'tensor'), may hold values from -2 to 2
- key_mantissa_block: bfloat16 [2, 2048, 1024], P('section', 'seq', 'tensor'), may hold values from -32 to 32
- key_exponent_scale: int32 [2, 2048, 32], P('section', 'seq', 'tensor'), may hold values from -2 to 2
- value_mantissa_block: bfloat16 [2, 2048, 1024], P('section', 'seq', 'tensor'), may hold values from -6 to 6
- value_exponent_scale: int32 [2, 2048, 32], P('section', 'seq', 'tensor'), may hold values from -1 to 1
- cached_key_rows: bfloat16 [2, 8, 4096, 128], P('section', 'tensor', 'seq'), may hold values from -12 to 12
- cached_value_rows: bfloat16 [2, 8, 4096, 128], P('section', 'tensor', 'seq'), may hold values from -8 to 8
- start: int32 [2], P('section'), may hold values from 2048 to 4096, as said below
Outputs:
- attended: bfloat16 [2, 2048, 16384], P('section', 'seq', 'tensor')
The draws below stay inside these ranges and needn't reach their ends.
Inputs may be any that keep to these rules, and one draw needn't show every extreme that they name: The first start[s] cached positions of section s hold earlier tokens; the cache of some section is full in every draw.
All inputs are finite; a program needn't handle non-finite values.
Results may differ from the reference program's by a relative error of at most 0.0023.
Values may be sent and summed in bfloat16 or wider, within the bound.
A program may use at most 64 MiB of HBM per device.

```python
import math
import jax
import jax.numpy as jnp
from jax import lax

QUERY_HEADS = 128
KEY_VALUE_HEADS = 8
HEAD_WIDTH = 128
RELAY_SECTIONS = 2
BLOCK_TOKENS = 2048
CACHED_POSITIONS = 4096


def exponent_lookup(key, feature_count):
    return jax.random.randint(key, (RELAY_SECTIONS, BLOCK_TOKENS, feature_count // 32), -2, 3, dtype=jnp.int32)


def draw_q_scale(key, part):
    return exponent_lookup(jax.random.fold_in(key, 101), QUERY_HEADS * HEAD_WIDTH)


def draw_key_exponent_scale(key, part):
    return exponent_lookup(jax.random.fold_in(key, 102), KEY_VALUE_HEADS * HEAD_WIDTH)


def mantissa_pair(key):
    q_base = jnp.clip(jax.random.normal(jax.random.fold_in(key, 211), (RELAY_SECTIONS, BLOCK_TOKENS, QUERY_HEADS * HEAD_WIDTH), jnp.float32), -6.0, 6.0)
    key_exponent_base = jnp.clip(jax.random.normal(jax.random.fold_in(key, 212), (RELAY_SECTIONS, BLOCK_TOKENS, KEY_VALUE_HEADS * HEAD_WIDTH), jnp.float32), -6.0, 6.0)
    return (q_base.astype(jnp.bfloat16), key_exponent_base.astype(jnp.bfloat16))


def draw_q_mant(key, part):
    return mantissa_pair(key)[0]


def draw_key_mantissa_block(key, part):
    return mantissa_pair(key)[1]


def draw_start(key, part):
    lowest = jax.random.randint(jax.random.fold_in(key, 301), (RELAY_SECTIONS,), CACHED_POSITIONS // 2, CACHED_POSITIONS + 1, dtype=jnp.int32)
    chosen = jax.random.randint(jax.random.fold_in(key, 302), (), 0, RELAY_SECTIONS, dtype=jnp.int32)
    return jnp.where(jnp.arange(RELAY_SECTIONS, dtype=jnp.int32) == chosen, CACHED_POSITIONS, lowest).astype(jnp.int32)


def touch_ends(values, stream_key, low, largest):
    longest = values.shape.index(max(values.shape))
    spots = []
    for shift in (0, 1):
        where = [jax.random.randint(jax.random.fold_in(stream_key, axis), (), 0, length) for axis, length in enumerate(values.shape)]
        where[longest] = (where[longest] + shift) % values.shape[longest]
        spots.append(tuple(where))
    return values.at[spots[0]].set(low).at[spots[1]].set(largest)


def steps_of(rng, dims, cuts, least, high):
    factor_of, own = 1.0, jax.random.fold_in(rng, 6)
    for position, blocks in cuts:
        steps = jnp.exp(jax.random.uniform(jax.random.fold_in(own, position), (blocks,), jnp.float32, least / len(cuts), high / len(cuts)))
        factor_of = factor_of * jnp.repeat(steps, dims[position] // blocks).reshape([-1 if axis == position else 1 for axis in range(len(dims))])
    return factor_of


def gaussian(own_key, extent, scale, reach, pieces=(), held_as=jnp.bfloat16):
    drawn = scale * jax.random.normal(own_key, extent, jnp.float32)
    if pieces:
        drawn = drawn * steps_of(own_key, extent, pieces, -0.22, 0.18)
    return jnp.clip(drawn, -reach, reach).astype(held_as)


def setup_inputs(seed: int = 0) -> dict:
    streams_of = jax.random.split(jax.random.key(seed), 10)
    return {
        "q_mant": draw_q_mant(jax.random.fold_in(streams_of[9], 71), 0),
        "q_scale": draw_q_scale(jax.random.fold_in(streams_of[9], 71), 0),
        "key_mantissa_block": draw_key_mantissa_block(jax.random.fold_in(streams_of[9], 71), 0),
        "key_exponent_scale": draw_key_exponent_scale(jax.random.fold_in(streams_of[9], 71), 0),
        "value_mantissa_block": gaussian(streams_of[4], (RELAY_SECTIONS, BLOCK_TOKENS, KEY_VALUE_HEADS * HEAD_WIDTH), 1.0, 6.0, ((0, 2), (1, 32), (2, 4))),
        "value_exponent_scale": touch_ends(jax.random.randint(streams_of[5], (RELAY_SECTIONS, BLOCK_TOKENS, KEY_VALUE_HEADS * HEAD_WIDTH // 32), -1, 2), jax.random.fold_in(streams_of[5], 1), -1, 1).astype(jnp.int32),
        "cached_key_rows": gaussian(streams_of[6], (RELAY_SECTIONS, KEY_VALUE_HEADS, CACHED_POSITIONS, HEAD_WIDTH), 2.0, 12.0, ((0, 2), (1, 4), (2, 32))),
        "cached_value_rows": gaussian(streams_of[7], (RELAY_SECTIONS, KEY_VALUE_HEADS, CACHED_POSITIONS, HEAD_WIDTH), 1.3, 8.0, ((0, 2), (1, 4), (2, 32))),
        "start": draw_start(jax.random.fold_in(streams_of[9], 71), 0),
    }


def decode_mantissas(mantissa, exponent):
    row_count, feature_count = mantissa.shape
    blocks = mantissa.astype(jnp.float32).reshape(row_count, feature_count // 32, 32)
    factor = jnp.exp2(exponent.astype(jnp.float32))[:, :, None]
    return (blocks * factor).reshape(row_count, feature_count).astype(jnp.bfloat16)

def reference(q_mant, q_scale, key_mantissa_block, key_exponent_scale, value_mantissa_block, value_exponent_scale, cached_key_rows, cached_value_rows, start):
    query_group_width = QUERY_HEADS // KEY_VALUE_HEADS
    inv_root = 1.0 / math.sqrt(HEAD_WIDTH)
    results = []
    for section_index in range(RELAY_SECTIONS):
        sender_section = (section_index - 1) % RELAY_SECTIONS
        queries = decode_mantissas(q_mant[sender_section], q_scale[sender_section]).reshape(BLOCK_TOKENS, QUERY_HEADS, HEAD_WIDTH)
        section_key_rows = decode_mantissas(key_mantissa_block[sender_section], key_exponent_scale[sender_section]).reshape(BLOCK_TOKENS, KEY_VALUE_HEADS, HEAD_WIDTH)
        section_value_rows = decode_mantissas(value_mantissa_block[sender_section], value_exponent_scale[sender_section]).reshape(BLOCK_TOKENS, KEY_VALUE_HEADS, HEAD_WIDTH)
        all_keys = jnp.concatenate([cached_key_rows[section_index], jnp.transpose(section_key_rows, (1, 0, 2))], axis=1)
        all_values = jnp.concatenate([cached_value_rows[section_index], jnp.transpose(section_value_rows, (1, 0, 2))], axis=1)
        cache_pos = jnp.arange(CACHED_POSITIONS, dtype=jnp.int32)
        query_pos = jnp.arange(BLOCK_TOKENS, dtype=jnp.int32)
        cache_ok = jnp.broadcast_to((cache_pos < start[section_index])[None, :], (BLOCK_TOKENS, CACHED_POSITIONS))
        span_ok = query_pos[None, :] <= query_pos[:, None]
        allowed = jnp.concatenate([cache_ok, span_ok], axis=1)

        def one_head(head_index):
            kv_head = head_index // query_group_width
            query_rows = lax.dynamic_index_in_dim(queries, head_index, 1, keepdims=False).astype(jnp.float32)
            head_keys = lax.dynamic_index_in_dim(all_keys, kv_head, 0, keepdims=False).astype(jnp.float32)
            head_values = lax.dynamic_index_in_dim(all_values, kv_head, 0, keepdims=False).astype(jnp.float32)
            scores = jnp.dot(query_rows, head_keys.T, preferred_element_type=jnp.float32) * inv_root
            scores = jnp.where(allowed, scores, -jnp.inf)
            row_max = lax.optimization_barrier(jnp.max(scores, axis=1, keepdims=True))
            weights = jnp.where(allowed, jnp.exp(scores - row_max), 0.0)
            row_total = lax.optimization_barrier(jnp.sum(weights, axis=1))
            rounded = lax.optimization_barrier(weights.astype(jnp.bfloat16)).astype(jnp.float32)
            mixed = jnp.dot(rounded, head_values, preferred_element_type=jnp.float32)
            return (mixed / row_total[:, None]).astype(jnp.bfloat16)
        heads_out = lax.map(one_head, jnp.arange(QUERY_HEADS, dtype=jnp.int32))
        results.append(jnp.transpose(heads_out, (1, 0, 2)).reshape(BLOCK_TOKENS, QUERY_HEADS * HEAD_WIDTH))
    return jnp.stack(results, axis=0)
```

```python
import math

import jax
import jax.numpy as jnp
from jax import lax
from jax.experimental import pallas as pl
from jax.experimental.pallas import tpu as pltpu
from jax.sharding import PartitionSpec as P

BF16, F32 = jnp.bfloat16, jnp.float32
MESH = pl.DeviceIdType.MESH
NX, NZ = 4, 8
HEAD = 128
GROUP_HEADS = 8
TOK = 64
CROWS = 128
ROWS = GROUP_HEADS * TOK
TILE = 128
NEAR = 3 * NX * CROWS
SCALE = (1.0 / math.sqrt(HEAD)) * math.log2(math.e)
NEG = -1e30
NT = (((1,), (1,)), ((), ()))
TN = (((0,), (0,)), ((), ()))


def spread(first, blocks, features):
    row = lax.broadcasted_iota(jnp.int32, (blocks, features), 0)
    col = lax.broadcasted_iota(jnp.int32, (blocks, features), 1)
    return jnp.where(row == first + col // 32, 1.0, 0.0).astype(BF16)


def kernel(
    q_hbm,
    q_scale,
    k_mant,
    k_scale,
    v_mant,
    v_scale,
    ck_hbm,
    cv_hbm,
    start,
    out,
    q_in,
    stage,
    qst,
    bst,
    qbuf,
    cb,
    bb,
    kp,
    vp,
    kb,
    vb,
    acc,
    top,
    bias,
    ost,
    load_sem,
    c_send,
    c_recv,
    b_send,
    b_recv,
    q_send,
    q_recv,
    o_send,
    o_recv,
    rc_send,
    rc_recv,
    sc_send,
    sc_recv,
    rb_send,
    rb_recv,
    sb_send,
    sb_recv,
):
    sec = lax.axis_index("section")
    seq = lax.axis_index("seq")
    ten = lax.axis_index("tensor")
    x, z = seq // NZ, seq % NZ
    yl, c = ten // 2, ten % 2
    other = 1 - sec
    step = 1 - 2 * c
    z_next = (z + step + NZ) % NZ

    def dev(s, xx, zz, cc):
        return {"section": s, "seq": xx * NZ + zz, "tensor": yl * 2 + cc}

    loads = [pltpu.make_async_copy(q_hbm, q_in, load_sem.at[4])]
    for i in range(2):
        loads.append(
            pltpu.make_async_copy(ck_hbm.at[i], stage.at[i, pl.ds(0, CROWS)], load_sem.at[2 * i])
        )
        loads.append(
            pltpu.make_async_copy(
                cv_hbm.at[i], stage.at[i, pl.ds(CROWS, CROWS)], load_sem.at[2 * i + 1]
            )
        )
    for cp in loads:
        cp.start()

    barrier = pltpu.get_barrier_semaphore()
    for ds in range(2):
        for dx in range(NX):
            for dc in range(2):
                if ds == 0 and dx == 0 and dc == 0:
                    continue
                pl.semaphore_signal(
                    barrier,
                    inc=1,
                    device_id=dev((sec + ds) % 2, (x + dx) % NX, z, (c + dc) % 2),
                    device_id_type=MESH,
                )
    for dz in (1, NZ - 1):
        pl.semaphore_signal(
            barrier, inc=1, device_id=dev(sec, x, (z + dz) % NZ, c), device_id_type=MESH
        )
    for cp in loads:
        cp.wait()
    pl.semaphore_wait(barrier, 17)

    def remote(src, dst, ssem, rsem, to):
        return pltpu.make_async_remote_copy(
            src_ref=src, dst_ref=dst, send_sem=ssem, recv_sem=rsem, device_id=to, device_id_type=MESH
        )

    def cache_piece(k):
        i, cc = k // 2, k % 2
        return remote(
            stage.at[i], cb.at[0, x], c_send.at[k], c_recv.at[x], dev(sec, 2 * c + i, z, cc)
        )

    def to_self(k):
        return jnp.logical_and(2 * c + k // 2 == x, k % 2 == c)

    for k in range(4):

        @pl.when(to_self(k))
        def _():
            pltpu.make_async_copy(stage.at[k // 2], cb.at[0, x], c_recv.at[x]).start()

        @pl.when(jnp.logical_not(to_self(k)))
        def _():
            cache_piece(k).start()

    q_factor = jnp.exp2(q_scale[...].astype(F32)).astype(BF16)

    def query_piece(r):
        k = (x + r) % NX
        return remote(
            qst.at[r], qbuf.at[x], q_send.at[r], q_recv.at[x], dev(other, 2 * c + k // 2, z, k % 2)
        )

    def send_queries(r):
        k = (x + r) % NX
        factor = jnp.dot(
            q_factor, spread(k * 32, q_factor.shape[1], 1024), preferred_element_type=F32
        )
        mant = q_in[:, pl.ds(pl.multiple_of(k * 1024, 1024), 1024)].astype(F32)
        decoded = (mant * factor).astype(BF16)
        for h in range(GROUP_HEADS):
            qst[r, pl.ds(h * TOK, TOK), :] = decoded[:, h * HEAD : (h + 1) * HEAD]
        query_piece(r).start()

    def block_piece(k):
        i, cc = k // 2, k % 2
        return remote(
            bst.at[i], bb.at[0, x], b_send.at[k], b_recv.at[x], dev(other, 2 * c + i, z, cc)
        )

    def send_block():
        for at, mant, scale in ((0, k_mant, k_scale), (TOK, v_mant, v_scale)):
            power = jnp.exp2(scale[...].astype(F32)).astype(BF16)
            factor = lax.dot_general(power, spread(0, 8, 256), TN, preferred_element_type=F32)
            decoded = (mant[...].astype(F32) * factor).astype(BF16)
            for i in range(2):
                bst[i, pl.ds(at, TOK), :] = decoded[:, i * HEAD : (i + 1) * HEAD]
        for k in range(4):
            block_piece(k).start()

    send_queries(0)
    send_block()
    for r in range(1, 4):
        send_queries(r)

    def slot(s):
        return 0 if s == 0 else (7 if s == 4 else 2 * s - 1 + c)

    def sib_slot(s):
        return 7 if s == 4 else 2 * s - c

    sibling = dev(sec, x, z, 1 - c)
    onward = dev(sec, x, z_next, c)

    def half(buf, n, hf):
        return buf.at[n, pl.ds(2 * hf, 2)]

    def hop(buf, s, hf, ssem, rsem):
        n = 0 if s == 4 else hf
        return remote(
            half(buf, slot(s - 1), hf), half(buf, slot(s), hf), ssem.at[s, n], rsem.at[s, n], onward
        )

    def across(buf, s, hf, ssem, rsem):
        n = 0 if s == 4 else hf
        return remote(
            half(buf, slot(s), hf), half(buf, slot(s), hf), ssem.at[s, n], rsem.at[s, n], sibling
        )

    def from_sibling(buf, s, hf, ssem, rsem):
        n = 0 if s == 4 else hf
        return remote(
            half(buf, sib_slot(s), hf), half(buf, sib_slot(s), hf), ssem.at[s, n], rsem.at[s, n], sibling
        )

    def halves(s):
        return (c,) if s == 4 else (0, 1)

    cache_ring = (cb, rc_send, rc_recv, sc_send, sc_recv)
    block_ring = (bb, rb_send, rb_recv, sb_send, sb_recv)

    def begin(ring, recv, width):
        buf, rs, rr, ss, sr = ring
        for hf in range(2):
            for xx in (2 * hf, 2 * hf + 1):
                remote(buf.at[0, xx], buf.at[0, xx], c_send.at[0], recv.at[xx], sibling).wait_recv()
            hop(buf, 1, hf, rs, rr).start()

    def forward(ring, s):
        buf, rs, rr, ss, sr = ring
        for hf in halves(s):
            hop(buf, s, hf, rs, rr).wait_recv()
            if s < 3:
                hop(buf, s + 1, hf, rs, rr).start()
            across(buf, s, hf, ss, sr).start()
        if s == 3:
            hop(buf, 4, c, rs, rr).start()

    def arrive(ring, s):
        buf, rs, rr, ss, sr = ring
        for hf in (1 - c,) if s == 4 else (0, 1):
            from_sibling(buf, s, hf, ss, sr).wait_recv()

    def drain(ring):
        buf, rs, rr, ss, sr = ring
        for s in range(1, 5):
            for hf in halves(s):
                hop(buf, s, hf, rs, rr).wait_send()
                across(buf, s, hf, ss, sr).wait_send()

    limit = start[0]

    def prepare(n, zz):
        for xx in range(NX):
            rows = pl.ds(n * NX * CROWS + xx * CROWS, CROWS)
            keys = cb[n, xx, pl.ds(0, CROWS), :]
            vals = cb[n, xx, pl.ds(CROWS, CROWS), :]
            ones = jnp.ones((CROWS, HEAD), BF16)
            if xx >= 2:
                at = xx * NZ * CROWS + zz * CROWS
                seen = at + lax.broadcasted_iota(jnp.int32, (CROWS, HEAD), 0) < limit
                keys = jnp.where(
                    seen, keys.astype(F32), cb[n, xx - 2, pl.ds(0, CROWS), :].astype(F32)
                ).astype(BF16)
                vals = jnp.where(seen, vals.astype(F32), 0.0).astype(BF16)
                ones = jnp.where(seen, 1.0, 0.0).astype(BF16)
            kp[rows, :] = keys
            vp[rows, pl.ds(0, HEAD)] = vals
            vp[rows, pl.ds(HEAD, HEAD)] = ones

    def prepare_pair(s):
        if s == 4:
            prepare(7, (z + 4) % NZ)
        else:
            prepare(2 * s - 1, (z - s + NZ) % NZ)
            prepare(2 * s, (z + s) % NZ)

    def prepare_block():
        for n in range(NZ):
            s = (n + 1) // 2
            zz = z if n == 0 else ((z + s) % NZ if n in (2, 4, 6, 7) else (z - s + NZ) % NZ)
            for xx in range(NX):
                rows = pl.ds(pl.multiple_of(xx * NZ * TOK + zz * TOK, TOK), TOK)
                kb[rows, :] = bb[n, xx, pl.ds(0, TOK), :]
                vb[rows, pl.ds(0, HEAD)] = bb[n, xx, pl.ds(TOK, TOK), :]

    def scores(g, t, keys):
        queries = qbuf[g, pl.ds(t * TILE, TILE), :]
        return lax.dot_general(queries, keys, NT, preferred_element_type=F32) * SCALE

    def near(g):
        tiles = range(ROWS // TILE)
        raw = [scores(g, t, kp[pl.ds(0, NEAR), :]) for t in tiles]
        for t in tiles:
            high = jnp.max(raw[t], axis=1, keepdims=True)
            weights = jnp.exp2(raw[t] - high).astype(BF16)
            acc[g, pl.ds(t * TILE, TILE), :] = jnp.dot(
                weights, vp[pl.ds(0, NEAR), :], preferred_element_type=F32
            )
            top[g, pl.ds(t * TILE, TILE), :] = jnp.broadcast_to(high, (TILE, HEAD))

    def rest(g):
        tiles = range(ROWS // TILE)
        far = pl.ds(NEAR, NX * NZ * CROWS - NEAR)
        diagonal = pl.ds(g * NZ * TOK, NZ * TOK)
        raw = []
        for t in tiles:
            parts = [scores(g, t, kp[far, :])]
            if g:
                parts.append(scores(g, t, kb[pl.ds(0, g * NZ * TOK), :]))
            parts.append(scores(g, t, kb[diagonal, :]) + bias[...])
            raw.append(parts)
        values = [vp.at[far]] + ([vb.at[pl.ds(0, g * NZ * TOK)]] if g else []) + [vb.at[diagonal]]
        for t in tiles:
            rows = pl.ds(t * TILE, TILE)
            old = top[g, rows, :]
            high = old
            for part in raw[t]:
                high = jnp.maximum(high, jnp.max(part, axis=1, keepdims=True))
            total = acc[g, rows, :] * jnp.exp2(old - high)[:, :1]
            for part, ref in zip(raw[t], values):
                weights = jnp.exp2(part - high[:, :1]).astype(BF16)
                total = total + jnp.dot(weights, ref[...], preferred_element_type=F32)
            done = (total[:, :HEAD] / total[:, HEAD:]).astype(BF16)
            for j in range(TILE // TOK):
                h = t * (TILE // TOK) + j
                ost[g, :, pl.ds(h * HEAD, HEAD)] = done[j * TOK : (j + 1) * TOK, :]

    def result_piece(g):
        p = 2 * (x % 2) + c
        return remote(
            ost.at[g],
            out.at[:, pl.ds(pl.multiple_of(p * 1024, 1024), 1024)],
            o_send.at[g],
            o_recv.at[p],
            dev(sec, g, z, x // 2),
        )

    def keep(g):
        return jnp.logical_and(g == x, x // 2 == c)

    def send_result(g):
        @pl.when(keep(g))
        def _():
            p = 2 * (x % 2) + c
            pltpu.make_async_copy(
                ost.at[g], out.at[:, pl.ds(pl.multiple_of(p * 1024, 1024), 1024)], o_recv.at[p]
            ).start()

        @pl.when(jnp.logical_not(keep(g)))
        def _():
            result_piece(g).start()

    def wait_queries(r):
        g = (2 * (x % 2) + c - r + NX) % NX
        remote(qbuf.at[g], qbuf.at[g], q_send.at[r], q_recv.at[g], sibling).wait_recv()
        return g

    row = lax.broadcasted_iota(jnp.int32, (TILE, NZ * TOK), 0) % TOK
    col = lax.broadcasted_iota(jnp.int32, (TILE, NZ * TOK), 1)
    bias[...] = jnp.where(col <= z * TOK + row, 0.0, NEG)
    vb[:, pl.ds(HEAD, HEAD)] = jnp.ones((NX * NZ * TOK, HEAD), BF16)

    begin(cache_ring, c_recv, CROWS)
    prepare(0, z)
    forward(cache_ring, 1)
    begin(block_ring, b_recv, TOK)
    arrive(cache_ring, 1)
    prepare_pair(1)
    near(wait_queries(0))
    forward(cache_ring, 2)
    forward(block_ring, 1)
    near(wait_queries(1))
    forward(cache_ring, 3)
    forward(block_ring, 2)
    near(wait_queries(2))
    forward(cache_ring, 4)
    forward(block_ring, 3)
    near(wait_queries(3))
    forward(block_ring, 4)
    for s in (2, 3, 4):
        arrive(cache_ring, s)
        prepare_pair(s)
    for s in (1, 2, 3, 4):
        arrive(block_ring, s)
    prepare_block()
    for g in (3, 2, 1, 0):
        rest(g)
        send_result(g)

    for k in range(4):

        @pl.when(jnp.logical_not(to_self(k)))
        def _():
            cache_piece(k).wait_send()

        block_piece(k).wait_send()
        query_piece(k).wait_send()
    drain(cache_ring)
    drain(block_ring)
    for g in range(4):

        @pl.when(jnp.logical_not(keep(g)))
        def _():
            result_piece(g).wait_send()

    for p in range(4):
        piece = out.at[:, pl.ds(p * 1024, 1024)]
        remote(piece, piece, o_send.at[p], o_recv.at[p], sibling).wait_recv()


def body(
    q_mant,
    q_scale,
    key_mantissa_block,
    key_exponent_scale,
    value_mantissa_block,
    value_exponent_scale,
    cached_key_rows,
    cached_value_rows,
    start,
):
    vmem = pl.BlockSpec(memory_space=pltpu.VMEM)
    anywhere = pl.BlockSpec(memory_space=pl.ANY)
    dma = pltpu.SemaphoreType.DMA
    result = pl.pallas_call(
        kernel,
        out_shape=jax.ShapeDtypeStruct((TOK, 4096), BF16),
        in_specs=[
            anywhere,
            vmem,
            vmem,
            vmem,
            vmem,
            vmem,
            anywhere,
            anywhere,
            pl.BlockSpec(memory_space=pltpu.SMEM),
        ],
        out_specs=vmem,
        scratch_shapes=[
            pltpu.VMEM((TOK, 4096), BF16),
            pltpu.VMEM((2, 2 * CROWS, HEAD), BF16),
            pltpu.VMEM((4, ROWS, HEAD), BF16),
            pltpu.VMEM((2, 2 * TOK, HEAD), BF16),
            pltpu.VMEM((NX, ROWS, HEAD), BF16),
            pltpu.VMEM((NZ, NX, 2 * CROWS, HEAD), BF16),
            pltpu.VMEM((NZ, NX, 2 * TOK, HEAD), BF16),
            pltpu.VMEM((NZ * NX * CROWS, HEAD), BF16),
            pltpu.VMEM((NZ * NX * CROWS, 2 * HEAD), BF16),
            pltpu.VMEM((NZ * NX * TOK, HEAD), BF16),
            pltpu.VMEM((NZ * NX * TOK, 2 * HEAD), BF16),
            pltpu.VMEM((NX, ROWS, 2 * HEAD), F32),
            pltpu.VMEM((NX, ROWS, HEAD), F32),
            pltpu.VMEM((TILE, NZ * TOK), F32),
            pltpu.VMEM((NX, TOK, 1024), BF16),
            dma((5,)),
        ]
        + [dma((4,))] * 8
        + [dma((5, 2))] * 8,
        compiler_params=pltpu.CompilerParams(
            collective_id=0, has_side_effects=True, vmem_limit_bytes=56 << 20
        ),
        name="attend",
    )(
        q_mant[0],
        q_scale[0],
        key_mantissa_block[0],
        jnp.swapaxes(key_exponent_scale[0], 0, 1),
        value_mantissa_block[0],
        jnp.swapaxes(value_exponent_scale[0], 0, 1),
        cached_key_rows[0],
        cached_value_rows[0],
        start,
    )
    return result[None]


def solution(mesh):
    return jax.shard_map(
        body,
        mesh=mesh,
        in_specs=(
            P("section", "seq", "tensor"),
            P("section", "seq", "tensor"),
            P("section", "seq", "tensor"),
            P("section", "seq", "tensor"),
            P("section", "seq", "tensor"),
            P("section", "seq", "tensor"),
            P("section", "tensor", "seq", None),
            P("section", "tensor", "seq", None),
            P("section"),
        ),
        out_specs=P("section", "seq", "tensor"),
        check_vma=False,
    )
```

```python
import functools
import math

import jax
import jax.numpy as jnp
from jax import lax
from jax.experimental import pallas as pl
from jax.experimental.pallas import tpu as pltpu
from jax.sharding import PartitionSpec as P

BF16, F32 = jnp.bfloat16, jnp.float32
MESH = pl.DeviceIdType.MESH
NX, NZ = 4, 8
HEAD = 128
GROUP_HEADS = 8
TOK = 64
CROWS = 128
ROWS = GROUP_HEADS * TOK
TILE = 128
CHUNK = NX * CROWS
SCALE = (1.0 / math.sqrt(HEAD)) * math.log2(math.e)
NEG = -1e30
NT = (((1,), (1,)), ((), ()))
TN = (((0,), (0,)), ((), ()))


def spread(first, blocks, features):
    row = lax.broadcasted_iota(jnp.int32, (blocks, features), 0)
    col = lax.broadcasted_iota(jnp.int32, (blocks, features), 1)
    return jnp.where(row == first + col // 32, 1.0, 0.0).astype(BF16)


def kernel(
    q_hbm,
    qs_hbm,
    km_hbm,
    ks_hbm,
    vm_hbm,
    vs_hbm,
    ck_hbm,
    cv_hbm,
    start,
    out,
    q_in,
    q_scale,
    k_mant,
    k_scale,
    v_mant,
    v_scale,
    stage,
    qst,
    bst,
    qbuf,
    cb,
    bb,
    kp,
    vp,
    kb,
    vb,
    acc,
    top,
    bias,
    ost,
    load_sem,
    c_send,
    c_recv,
    b_send,
    b_recv,
    q_send,
    q_recv,
    o_send,
    o_recv,
    rc_send,
    rc_recv,
    sc_send,
    sc_recv,
    rb_send,
    rb_recv,
    sb_send,
    sb_recv,
):
    sec = lax.axis_index("section")
    seq = lax.axis_index("seq")
    ten = lax.axis_index("tensor")
    x, z = seq // NZ, seq % NZ
    yl, c = ten // 2, ten % 2
    other = 1 - sec

    def dev(s, xx, zz, cc):
        return {"section": s, "seq": xx * NZ + zz, "tensor": yl * 2 + cc}

    loads = []
    for i in range(2):
        loads.append((ck_hbm.at[i], stage.at[i, pl.ds(0, CROWS)]))
        loads.append((cv_hbm.at[i], stage.at[i, pl.ds(CROWS, CROWS)]))
    loads += [(q_hbm, q_in), (qs_hbm, q_scale), (km_hbm, k_mant), (ks_hbm, k_scale)]
    loads += [(vm_hbm, v_mant), (vs_hbm, v_scale)]
    loads = [pltpu.make_async_copy(a, b, load_sem.at[n]) for n, (a, b) in enumerate(loads)]
    for cp in loads:
        cp.start()

    barrier = pltpu.get_barrier_semaphore()
    for ds in range(2):
        for dx in range(NX):
            for dc in range(2):
                if ds == 0 and dx == 0 and dc == 0:
                    continue
                pl.semaphore_signal(
                    barrier,
                    inc=1,
                    device_id=dev((sec + ds) % 2, (x + dx) % NX, z, (c + dc) % 2),
                    device_id_type=MESH,
                )
    for dz in (1, NZ - 1):
        pl.semaphore_signal(
            barrier, inc=1, device_id=dev(sec, x, (z + dz) % NZ, c), device_id_type=MESH
        )
    for cp in loads[:4]:
        cp.wait()
    pl.semaphore_wait(barrier, 17)

    def remote(src, dst, ssem, rsem, to):
        return pltpu.make_async_remote_copy(
            src_ref=src, dst_ref=dst, send_sem=ssem, recv_sem=rsem, device_id=to, device_id_type=MESH
        )

    def cache_piece(k):
        i, cc = k // 2, k % 2
        return remote(
            stage.at[i], cb.at[0, x], c_send.at[k], c_recv.at[x], dev(sec, 2 * c + i, z, cc)
        )

    def to_self(k):
        return jnp.logical_and(2 * c + k // 2 == x, k % 2 == c)

    for k in range(4):

        @pl.when(to_self(k))
        def _():
            pltpu.make_async_copy(stage.at[k // 2], cb.at[0, x], c_recv.at[x]).start()

        @pl.when(jnp.logical_not(to_self(k)))
        def _():
            cache_piece(k).start()

    for cp in loads[4:]:
        cp.wait()

    q_factor = jnp.exp2(q_scale[...].astype(F32)).astype(BF16)

    def query_piece(r):
        k = (x + r) % NX
        return remote(
            qst.at[r], qbuf.at[x], q_send.at[r], q_recv.at[x], dev(other, 2 * c + k // 2, z, k % 2)
        )

    def send_queries(r):
        k = (x + r) % NX
        factor = jnp.dot(
            q_factor, spread(k * 32, q_factor.shape[1], 1024), preferred_element_type=F32
        )
        mant = q_in[:, pl.ds(pl.multiple_of(k * 1024, 1024), 1024)].astype(F32)
        decoded = (mant * factor).astype(BF16)
        for h in range(GROUP_HEADS):
            qst[r, pl.ds(h * TOK, TOK), :] = decoded[:, h * HEAD : (h + 1) * HEAD]
        query_piece(r).start()

    def block_piece(k):
        i, cc = k // 2, k % 2
        return remote(
            bst.at[i], bb.at[0, x], b_send.at[k], b_recv.at[x], dev(other, 2 * c + i, z, cc)
        )

    def send_block():
        for at, mant, scale in ((0, k_mant, k_scale), (TOK, v_mant, v_scale)):
            power = jnp.exp2(scale[...].astype(F32)).astype(BF16)
            factor = lax.dot_general(power, spread(0, 8, 256), TN, preferred_element_type=F32)
            decoded = (mant[...].astype(F32) * factor).astype(BF16)
            for i in range(2):
                bst[i, pl.ds(at, TOK), :] = decoded[:, i * HEAD : (i + 1) * HEAD]
        for k in range(4):
            block_piece(k).start()

    send_queries(0)
    send_block()
    for r in range(1, 4):
        send_queries(r)

    sibling = dev(sec, x, z, 1 - c)
    onward = (dev(sec, x, (z + 1) % NZ, c), dev(sec, x, (z + NZ - 1) % NZ, c))

    def slot(s, d):
        return 0 if s == 0 else (7 if s == 4 else 2 * s - 1 + d)

    def unit(buf, n, s, d, core):
        return buf.at[n, pl.ds(2 * core + d, 1) if s == 4 else pl.ds(2 * core, 2)]

    def hop(ring, s, d):
        buf, rs, rr = ring[:3]
        src, dst = unit(buf, slot(s - 1, d), s, d, c), unit(buf, slot(s, d), s, d, c)
        return remote(src, dst, rs.at[s, d], rr.at[s, d], onward[d])

    def across(ring, s, d):
        here = unit(ring[0], slot(s, d), s, d, c)
        return remote(here, here, ring[3].at[s, d], ring[4].at[s, d], sibling)

    def from_sibling(ring, s, d):
        here = unit(ring[0], slot(s, d), s, d, 1 - c)
        return remote(here, here, ring[3].at[s, d], ring[4].at[s, d], sibling)

    cache_ring = (cb, rc_send, rc_recv, sc_send, sc_recv)
    block_ring = (bb, rb_send, rb_recv, sb_send, sb_recv)

    def own(ring, recv, core):
        for n in range(2):
            here = ring[0].at[0, 2 * core + n]
            remote(here, here, c_send.at[0], recv.at[2 * core + n], sibling).wait_recv()

    def begin(ring, recv):
        own(ring, recv, c)
        for d in range(2):
            hop(ring, 1, d).start()

    def forward(ring, s):
        for d in range(2):
            hop(ring, s, d).wait_recv()
            if s < 4:
                hop(ring, s + 1, d).start()
            across(ring, s, d).start()

    def arrive(ring, s):
        for d in range(2):
            from_sibling(ring, s, d).wait_recv()

    def drain(ring):
        for s in range(1, 5):
            for d in range(2):
                hop(ring, s, d).wait_send()
                across(ring, s, d).wait_send()

    limit = start[0]

    def prepare(n, zz):
        for xx in range(NX):
            rows = pl.ds(n * NX * CROWS + xx * CROWS, CROWS)
            keys = cb[n, xx, pl.ds(0, CROWS), :]
            vals = cb[n, xx, pl.ds(CROWS, CROWS), :]
            ones = jnp.ones((CROWS, HEAD), BF16)
            if xx >= 2:
                at = xx * NZ * CROWS + zz * CROWS
                seen = at + lax.broadcasted_iota(jnp.int32, (CROWS, HEAD), 0) < limit
                keys = jnp.where(
                    seen, keys.astype(F32), cb[n, xx - 2, pl.ds(0, CROWS), :].astype(F32)
                ).astype(BF16)
                vals = jnp.where(seen, vals.astype(F32), 0.0).astype(BF16)
                ones = jnp.where(seen, 1.0, 0.0).astype(BF16)
            kp[rows, :] = keys
            vp[rows, pl.ds(0, HEAD)] = vals
            vp[rows, pl.ds(HEAD, HEAD)] = ones

    def prepare_pair(s):
        if s == 4:
            prepare(7, (z + 4) % NZ)
        else:
            prepare(2 * s - 1, (z - s + NZ) % NZ)
            prepare(2 * s, (z + s) % NZ)

    def prepare_block():
        for n in range(NZ):
            s = (n + 1) // 2
            zz = z if n == 0 else ((z + s) % NZ if n in (2, 4, 6, 7) else (z - s + NZ) % NZ)
            for xx in range(NX):
                rows = pl.ds(pl.multiple_of(xx * NZ * TOK + zz * TOK, TOK), TOK)
                kb[rows, :] = bb[n, xx, pl.ds(0, TOK), :]
                vb[rows, pl.ds(0, HEAD)] = bb[n, xx, pl.ds(TOK, TOK), :]

    def scores(g, t, keys):
        queries = qbuf[g, pl.ds(t * TILE, TILE), :]
        return lax.dot_general(queries, keys, NT, preferred_element_type=F32) * SCALE

    tiles = range(ROWS // TILE)

    def first(g):
        keys = pl.ds(0, CHUNK)
        raw = [scores(g, t, kp[keys, :]) for t in tiles]
        for t in tiles:
            rows = pl.ds(t * TILE, TILE)
            high = jnp.max(raw[t], axis=1, keepdims=True)
            weights = jnp.exp2(raw[t] - high).astype(BF16)
            acc[g, rows, :] = jnp.dot(weights, vp[keys, :], preferred_element_type=F32)
            top[g, rows, :] = jnp.broadcast_to(high, (TILE, HEAD))

    def update(g, t, parts, values):
        rows = pl.ds(t * TILE, TILE)
        old = top[g, rows, :]
        high = old
        for part in parts:
            high = jnp.maximum(high, jnp.max(part, axis=1, keepdims=True))
        total = acc[g, rows, :] * jnp.exp2(old - high)[:, :1]
        for part, ref in zip(parts, values):
            weights = jnp.exp2(part - high[:, :1]).astype(BF16)
            total = total + jnp.dot(weights, ref[...], preferred_element_type=F32)
        return high, total

    def pair(g, s):
        keys = pl.ds((2 * s - 1) * CHUNK, 2 * CHUNK)
        raw = [[scores(g, t, kp[keys, :])] for t in tiles]
        for t in tiles:
            rows = pl.ds(t * TILE, TILE)
            high, total = update(g, t, raw[t], [vp.at[keys]])
            acc[g, rows, :] = total
            top[g, rows, :] = high

    def last(g):
        far = pl.ds(7 * CHUNK, CHUNK)
        whole = pl.ds(0, g * NZ * TOK)
        diagonal = pl.ds(g * NZ * TOK, NZ * TOK)
        raw = []
        for t in tiles:
            parts = [scores(g, t, kp[far, :])]
            if g:
                parts.append(scores(g, t, kb[whole, :]))
            parts.append(scores(g, t, kb[diagonal, :]) + bias[...])
            raw.append(parts)
        values = [vp.at[far]] + ([vb.at[whole]] if g else []) + [vb.at[diagonal]]
        for t in tiles:
            high, total = update(g, t, raw[t], values)
            done = (total[:, :HEAD] / total[:, HEAD:]).astype(BF16)
            for j in range(TILE // TOK):
                h = t * (TILE // TOK) + j
                ost[g, :, pl.ds(h * HEAD, HEAD)] = done[j * TOK : (j + 1) * TOK, :]

    def result_piece(g):
        p = 2 * (x % 2) + c
        return remote(
            ost.at[g],
            out.at[:, pl.ds(pl.multiple_of(p * 1024, 1024), 1024)],
            o_send.at[g],
            o_recv.at[p],
            dev(sec, g, z, x // 2),
        )

    def keep(g):
        return jnp.logical_and(g == x, x // 2 == c)

    def send_result(g):
        @pl.when(keep(g))
        def _():
            p = 2 * (x % 2) + c
            pltpu.make_async_copy(
                ost.at[g], out.at[:, pl.ds(pl.multiple_of(p * 1024, 1024), 1024)], o_recv.at[p]
            ).start()

        @pl.when(jnp.logical_not(keep(g)))
        def _():
            result_piece(g).start()

    def wait_queries(r):
        g = (2 * (x % 2) + c - r + NX) % NX
        remote(qbuf.at[g], qbuf.at[g], q_send.at[r], q_recv.at[g], sibling).wait_recv()
        return g

    row = lax.broadcasted_iota(jnp.int32, (TILE, NZ * TOK), 0) % TOK
    col = lax.broadcasted_iota(jnp.int32, (TILE, NZ * TOK), 1)
    bias[...] = jnp.where(col <= z * TOK + row, 0.0, NEG)
    vb[:, pl.ds(HEAD, HEAD)] = jnp.ones((NX * NZ * TOK, HEAD), BF16)

    begin(cache_ring, c_recv)
    begin(block_ring, b_recv)
    own(cache_ring, c_recv, 1 - c)
    own(block_ring, b_recv, 1 - c)
    prepare(0, z)
    order = [wait_queries(0)]
    first(order[0])
    order.append(wait_queries(1))
    first(order[1])
    forward(cache_ring, 1)
    order.append(wait_queries(2))
    first(order[2])
    forward(block_ring, 1)
    arrive(cache_ring, 1)
    prepare_pair(1)
    pair(order[0], 1)
    pair(order[1], 1)
    order.append(wait_queries(3))
    first(order[3])
    for s in (1, 2, 3):
        if s > 1:
            arrive(cache_ring, s)
            prepare_pair(s)
            pair(order[0], s)
            pair(order[1], s)
        forward(cache_ring, s + 1)
        pair(order[2], s)
        forward(block_ring, s + 1)
        pair(order[3], s)
    arrive(cache_ring, 4)
    prepare_pair(4)
    for s in (1, 2, 3, 4):
        arrive(block_ring, s)
    prepare_block()

    def finish(r, carry):
        g = (x + r + 1) % NX
        for n in range(NX):
            pl.when(g == n)(functools.partial(last, n))
        send_result(g)
        return carry

    lax.fori_loop(0, NX, finish, 0)

    for k in range(4):

        @pl.when(jnp.logical_not(to_self(k)))
        def _():
            cache_piece(k).wait_send()

        block_piece(k).wait_send()
        query_piece(k).wait_send()
    drain(cache_ring)
    drain(block_ring)
    for g in range(4):

        @pl.when(jnp.logical_not(keep(g)))
        def _():
            result_piece(g).wait_send()

    for p in range(4):
        piece = out.at[:, pl.ds(p * 1024, 1024)]
        remote(piece, piece, o_send.at[p], o_recv.at[p], sibling).wait_recv()


def body(
    q_mant,
    q_scale,
    key_mantissa_block,
    key_exponent_scale,
    value_mantissa_block,
    value_exponent_scale,
    cached_key_rows,
    cached_value_rows,
    start,
):
    vmem = pl.BlockSpec(memory_space=pltpu.VMEM)
    anywhere = pl.BlockSpec(memory_space=pl.ANY)
    dma = pltpu.SemaphoreType.DMA
    result = pl.pallas_call(
        kernel,
        out_shape=pltpu.VMEM((TOK, 4096), BF16),
        in_specs=[
            *[anywhere] * 8,
            pl.BlockSpec(memory_space=pltpu.SMEM),
        ],
        out_specs=vmem,
        scratch_shapes=[
            pltpu.VMEM((TOK, 4096), BF16),
            pltpu.VMEM((TOK, 128), jnp.int32),
            pltpu.VMEM((TOK, 256), BF16),
            pltpu.VMEM((8, TOK), jnp.int32),
            pltpu.VMEM((TOK, 256), BF16),
            pltpu.VMEM((8, TOK), jnp.int32),
            pltpu.VMEM((2, 2 * CROWS, HEAD), BF16),
            pltpu.VMEM((4, ROWS, HEAD), BF16),
            pltpu.VMEM((2, 2 * TOK, HEAD), BF16),
            pltpu.VMEM((NX, ROWS, HEAD), BF16),
            pltpu.VMEM((NZ, NX, 2 * CROWS, HEAD), BF16),
            pltpu.VMEM((NZ, NX, 2 * TOK, HEAD), BF16),
            pltpu.VMEM((NZ * NX * CROWS, HEAD), BF16),
            pltpu.VMEM((NZ * NX * CROWS, 2 * HEAD), BF16),
            pltpu.VMEM((NZ * NX * TOK, HEAD), BF16),
            pltpu.VMEM((NZ * NX * TOK, 2 * HEAD), BF16),
            pltpu.VMEM((NX, ROWS, 2 * HEAD), F32),
            pltpu.VMEM((NX, ROWS, HEAD), F32),
            pltpu.VMEM((TILE, NZ * TOK), F32),
            pltpu.VMEM((NX, TOK, 1024), BF16),
            dma((10,)),
        ]
        + [dma((4,))] * 8
        + [dma((5, 2))] * 8,
        compiler_params=pltpu.CompilerParams(
            collective_id=0, has_side_effects=True, vmem_limit_bytes=56 << 20
        ),
        name="attend",
    )(
        q_mant[0],
        q_scale[0],
        key_mantissa_block[0],
        jnp.swapaxes(key_exponent_scale[0], 0, 1),
        value_mantissa_block[0],
        jnp.swapaxes(value_exponent_scale[0], 0, 1),
        cached_key_rows[0],
        cached_value_rows[0],
        start,
    )
    return result[None]


def solution(mesh):
    return jax.shard_map(
        body,
        mesh=mesh,
        in_specs=(
            P("section", "seq", "tensor"),
            P("section", "seq", "tensor"),
            P("section", "seq", "tensor"),
            P("section", "seq", "tensor"),
            P("section", "seq", "tensor"),
            P("section", "seq", "tensor"),
            P("section", "tensor", "seq", None),
            P("section", "tensor", "seq", None),
            P("section"),
        ),
        out_specs=P("section", "seq", "tensor"),
        check_vma=False,
    )
```

```python
import functools
import math

import jax
import jax.numpy as jnp
from jax import lax
from jax.experimental import pallas as pl
from jax.experimental.pallas import tpu as pltpu
from jax.sharding import PartitionSpec as P

BF16, F32 = jnp.bfloat16, jnp.float32
MESH = pl.DeviceIdType.MESH
NX, NZ = 4, 8
HEAD = 128
GROUP_HEADS = 8
TOK = 64
CROWS = 128
ROWS = GROUP_HEADS * TOK
TILE = 128
CHUNK = NX * CROWS
SCALE = (1.0 / math.sqrt(HEAD)) * math.log2(math.e)
NEG = -1e30
NT = (((1,), (1,)), ((), ()))
TN = (((0,), (0,)), ((), ()))


def spread(first, blocks, features):
    row = lax.broadcasted_iota(jnp.int32, (blocks, features), 0)
    col = lax.broadcasted_iota(jnp.int32, (blocks, features), 1)
    return jnp.where(row == first + col // 32, 1.0, 0.0).astype(BF16)


def kernel(
    q_hbm,
    qs_hbm,
    km_hbm,
    ks_hbm,
    vm_hbm,
    vs_hbm,
    ck_hbm,
    cv_hbm,
    start,
    out,
    q_in,
    q_scale,
    k_mant,
    k_scale,
    v_mant,
    v_scale,
    stage,
    qst,
    bst,
    qbuf,
    cb,
    bb,
    kp,
    vp,
    kb,
    vb,
    acc,
    top,
    bias,
    ost,
    load_sem,
    c_send,
    c_recv,
    n_send,
    n_recv,
    b_send,
    b_recv,
    q_send,
    q_recv,
    o_send,
    o_recv,
    rc_send,
    rc_recv,
    sc_send,
    sc_recv,
    rb_send,
    rb_recv,
    sb_send,
    sb_recv,
):
    sec = lax.axis_index("section")
    seq = lax.axis_index("seq")
    ten = lax.axis_index("tensor")
    x, z = seq // NZ, seq % NZ
    yl, c = ten // 2, ten % 2
    other = 1 - sec

    def dev(s, xx, zz, cc):
        return {"section": s, "seq": xx * NZ + zz, "tensor": yl * 2 + cc}

    loads = []
    for i in range(2):
        loads.append((ck_hbm.at[i], stage.at[i, pl.ds(0, CROWS)]))
        loads.append((cv_hbm.at[i], stage.at[i, pl.ds(CROWS, CROWS)]))
    loads += [(q_hbm, q_in), (qs_hbm, q_scale), (km_hbm, k_mant), (ks_hbm, k_scale)]
    loads += [(vm_hbm, v_mant), (vs_hbm, v_scale)]
    loads = [pltpu.make_async_copy(a, b, load_sem.at[n]) for n, (a, b) in enumerate(loads)]
    for cp in loads:
        cp.start()

    barrier = pltpu.get_barrier_semaphore()
    for ds in range(2):
        for dx in range(NX):
            for dc in range(2):
                if ds == 0 and dx == 0 and dc == 0:
                    continue
                pl.semaphore_signal(
                    barrier,
                    inc=1,
                    device_id=dev((sec + ds) % 2, (x + dx) % NX, z, (c + dc) % 2),
                    device_id_type=MESH,
                )
    for dz in (1, NZ - 1):
        zz = (z + dz) % NZ
        for to in (dev(sec, x, zz, c), dev(sec, 2 * c, zz, x // 2), dev(sec, 2 * c + 1, zz, x // 2)):
            pl.semaphore_signal(barrier, inc=1, device_id=to, device_id_type=MESH)
    for cp in loads[:4]:
        cp.wait()
    pl.semaphore_wait(barrier, 21)

    def remote(src, dst, ssem, rsem, to):
        return pltpu.make_async_remote_copy(
            src_ref=src, dst_ref=dst, send_sem=ssem, recv_sem=rsem, device_id=to, device_id_type=MESH
        )

    def cache_piece(k):
        i, cc = k // 2, k % 2
        return remote(
            stage.at[i], cb.at[0, x], c_send.at[k], c_recv.at[x], dev(sec, 2 * c + i, z, cc)
        )

    def to_self(k):
        return jnp.logical_and(2 * c + k // 2 == x, k % 2 == c)

    for k in range(4):

        @pl.when(to_self(k))
        def _():
            pltpu.make_async_copy(stage.at[k // 2], cb.at[0, x], c_recv.at[x]).start()

        @pl.when(jnp.logical_not(to_self(k)))
        def _():
            cache_piece(k).start()

    def near_piece(i, d):
        zz = (z + (1, NZ - 1)[d]) % NZ
        return remote(
            stage.at[i],
            cb.at[1 + d, x],
            n_send.at[d, i],
            n_recv.at[d, x % 2],
            dev(sec, 2 * c + i, zz, x // 2),
        )

    for i in range(2):
        for d in range(2):
            near_piece(i, d).start()

    for cp in loads[4:]:
        cp.wait()

    q_factor = jnp.exp2(q_scale[...].astype(F32)).astype(BF16)

    def query_piece(r):
        k = (x + r) % NX
        return remote(
            qst.at[r], qbuf.at[x], q_send.at[r], q_recv.at[x], dev(other, 2 * c + k // 2, z, k % 2)
        )

    def decode_queries(r):
        k = (x + r) % NX
        factor = jnp.dot(
            q_factor, spread(k * 32, q_factor.shape[1], 1024), preferred_element_type=F32
        )
        mant = q_in[:, pl.ds(pl.multiple_of(k * 1024, 1024), 1024)].astype(F32)
        decoded = (mant * factor).astype(BF16)
        for h in range(GROUP_HEADS):
            qst[r, pl.ds(h * TOK, TOK), :] = decoded[:, h * HEAD : (h + 1) * HEAD]

    def next_queries(r):
        query_piece(r - 1).wait_send()
        query_piece(r).start()

    def block_piece(k):
        i, cc = k // 2, k % 2
        return remote(
            bst.at[i], bb.at[0, x], b_send.at[k], b_recv.at[x], dev(other, 2 * c + i, z, cc)
        )

    def send_block():
        for at, mant, scale in ((0, k_mant, k_scale), (TOK, v_mant, v_scale)):
            power = jnp.exp2(scale[...].astype(F32)).astype(BF16)
            factor = lax.dot_general(power, spread(0, 8, 256), TN, preferred_element_type=F32)
            decoded = (mant[...].astype(F32) * factor).astype(BF16)
            for i in range(2):
                bst[i, pl.ds(at, TOK), :] = decoded[:, i * HEAD : (i + 1) * HEAD]
        for k in range(4):
            block_piece(k).start()

    decode_queries(0)
    query_piece(0).start()
    send_block()
    for r in range(1, 4):
        decode_queries(r)

    sibling = dev(sec, x, z, 1 - c)
    onward = (dev(sec, x, (z + 1) % NZ, c), dev(sec, x, (z + NZ - 1) % NZ, c))

    def slot(s, d):
        return 0 if s == 0 else (7 if s == 4 else 2 * s - 1 + d)

    def unit(buf, n, s, d, core):
        return buf.at[n, pl.ds(2 * core + d, 1) if s == 4 else pl.ds(2 * core, 2)]

    def hop(ring, s, d):
        buf, rs, rr = ring[:3]
        src, dst = unit(buf, slot(s - 1, d), s, d, c), unit(buf, slot(s, d), s, d, c)
        return remote(src, dst, rs.at[s, d], rr.at[s, d], onward[d])

    def across(ring, s, d):
        here = unit(ring[0], slot(s, d), s, d, c)
        return remote(here, here, ring[3].at[s, d], ring[4].at[s, d], sibling)

    def from_sibling(ring, s, d):
        here = unit(ring[0], slot(s, d), s, d, 1 - c)
        return remote(here, here, ring[3].at[s, d], ring[4].at[s, d], sibling)

    cache_ring = (cb, rc_send, rc_recv, sc_send, sc_recv)
    block_ring = (bb, rb_send, rb_recv, sb_send, sb_recv)

    def own(ring, recv, core):
        for n in range(2):
            here = ring[0].at[0, 2 * core + n]
            remote(here, here, c_send.at[0], recv.at[2 * core + n], sibling).wait_recv()

    def begin_block():
        own(block_ring, b_recv, c)
        for d in range(2):
            hop(block_ring, 1, d).start()

    def forward(ring, s):
        for d in range(2):
            if s == 1 and ring is cache_ring:
                for n in range(2):
                    here = cb.at[1 + d, 2 * c + n]
                    remote(here, here, n_send.at[d, n], n_recv.at[d, n], sibling).wait_recv()
            else:
                hop(ring, s, d).wait_recv()
            if s < 4:
                hop(ring, s + 1, d).start()
            across(ring, s, d).start()

    def arrive(ring, s):
        for d in range(2):
            from_sibling(ring, s, d).wait_recv()

    def drain(ring):
        for s in range(1, 5):
            for d in range(2):
                if s > 1 or ring is block_ring:
                    hop(ring, s, d).wait_send()
                across(ring, s, d).wait_send()

    limit = start[0]

    def prepare(n, zz):
        for xx in range(NX):
            rows = pl.ds(n * NX * CROWS + xx * CROWS, CROWS)
            keys = cb[n, xx, pl.ds(0, CROWS), :]
            vals = cb[n, xx, pl.ds(CROWS, CROWS), :]
            ones = jnp.ones((CROWS, HEAD), BF16)
            if xx >= 2:
                at = xx * NZ * CROWS + zz * CROWS
                seen = at + lax.broadcasted_iota(jnp.int32, (CROWS, HEAD), 0) < limit
                keys = jnp.where(
                    seen, keys.astype(F32), cb[n, xx - 2, pl.ds(0, CROWS), :].astype(F32)
                ).astype(BF16)
                vals = jnp.where(seen, vals.astype(F32), 0.0).astype(BF16)
                ones = jnp.where(seen, 1.0, 0.0).astype(BF16)
            kp[rows, :] = keys
            vp[rows, pl.ds(0, HEAD)] = vals
            vp[rows, pl.ds(HEAD, HEAD)] = ones

    def prepare_pair(s):
        if s == 4:
            prepare(7, (z + 4) % NZ)
        else:
            prepare(2 * s - 1, (z - s + NZ) % NZ)
            prepare(2 * s, (z + s) % NZ)

    def prepare_block():
        for n in range(NZ):
            s = (n + 1) // 2
            zz = z if n == 0 else ((z + s) % NZ if n in (2, 4, 6, 7) else (z - s + NZ) % NZ)
            for xx in range(NX):
                rows = pl.ds(pl.multiple_of(xx * NZ * TOK + zz * TOK, TOK), TOK)
                kb[rows, :] = bb[n, xx, pl.ds(0, TOK), :]
                vb[rows, pl.ds(0, HEAD)] = bb[n, xx, pl.ds(TOK, TOK), :]

    def scores(g, t, keys):
        queries = qbuf[g, pl.ds(t * TILE, TILE), :]
        return lax.dot_general(queries, keys, NT, preferred_element_type=F32) * SCALE

    tiles = range(ROWS // TILE)

    def wide(a, width):
        return jnp.tile(a, (1, width // HEAD))

    def first(g):
        keys = pl.ds(0, CHUNK)
        raw = [scores(g, t, kp[keys, :]) for t in tiles]
        for t in tiles:
            rows = pl.ds(t * TILE, TILE)
            high = jnp.broadcast_to(jnp.max(raw[t], axis=1, keepdims=True), (TILE, HEAD))
            weights = jnp.exp2(raw[t] - wide(high, CHUNK)).astype(BF16)
            acc[g, rows, :] = jnp.dot(weights, vp[keys, :], preferred_element_type=F32)
            top[g, rows, :] = high

    def update(g, t, parts, values):
        rows = pl.ds(t * TILE, TILE)
        peak = jnp.max(parts[0], axis=1, keepdims=True)
        for part in parts[1:]:
            peak = jnp.maximum(peak, jnp.max(part, axis=1, keepdims=True))
        old = top[g, rows, :]
        high = jnp.maximum(old, jnp.broadcast_to(peak, (TILE, HEAD)))
        total = acc[g, rows, :] * wide(jnp.exp2(old - high), 2 * HEAD)
        for part, ref in zip(parts, values):
            weights = jnp.exp2(part - wide(high, part.shape[1])).astype(BF16)
            total = total + jnp.dot(weights, ref[...], preferred_element_type=F32)
        return high, total

    def pair(g, s):
        keys = pl.ds((2 * s - 1) * CHUNK, 2 * CHUNK)
        raw = [[scores(g, t, kp[keys, :])] for t in tiles]
        for t in tiles:
            rows = pl.ds(t * TILE, TILE)
            high, total = update(g, t, raw[t], [vp.at[keys]])
            acc[g, rows, :] = total
            top[g, rows, :] = high

    def last(g):
        far = pl.ds(7 * CHUNK, CHUNK)
        whole = pl.ds(0, g * NZ * TOK)
        diagonal = pl.ds(g * NZ * TOK, NZ * TOK)
        raw = []
        for t in tiles:
            parts = [scores(g, t, kp[far, :])]
            if g:
                parts.append(scores(g, t, kb[whole, :]))
            parts.append(scores(g, t, kb[diagonal, :]) + bias[...])
            raw.append(parts)
        values = [vp.at[far]] + ([vb.at[whole]] if g else []) + [vb.at[diagonal]]
        for t in tiles:
            high, total = update(g, t, raw[t], values)
            done = (total[:, :HEAD] / total[:, HEAD:]).astype(BF16)
            for j in range(TILE // TOK):
                h = t * (TILE // TOK) + j
                ost[g, :, pl.ds(h * HEAD, HEAD)] = done[j * TOK : (j + 1) * TOK, :]

    def result_piece(g):
        p = 2 * (x % 2) + c
        return remote(
            ost.at[g],
            out.at[:, pl.ds(pl.multiple_of(p * 1024, 1024), 1024)],
            o_send.at[g],
            o_recv.at[p],
            dev(sec, g, z, x // 2),
        )

    def keep(g):
        return jnp.logical_and(g == x, x // 2 == c)

    def send_result(g):
        @pl.when(keep(g))
        def _():
            p = 2 * (x % 2) + c
            pltpu.make_async_copy(
                ost.at[g], out.at[:, pl.ds(pl.multiple_of(p * 1024, 1024), 1024)], o_recv.at[p]
            ).start()

        @pl.when(jnp.logical_not(keep(g)))
        def _():
            result_piece(g).start()

    def wait_queries(r):
        g = (2 * (x % 2) + c - r + NX) % NX
        remote(qbuf.at[g], qbuf.at[g], q_send.at[r], q_recv.at[g], sibling).wait_recv()
        return g

    row = lax.broadcasted_iota(jnp.int32, (TILE, NZ * TOK), 0) % TOK
    col = lax.broadcasted_iota(jnp.int32, (TILE, NZ * TOK), 1)
    bias[...] = jnp.where(col <= z * TOK + row, 0.0, NEG)
    vb[:, pl.ds(HEAD, HEAD)] = jnp.ones((NX * NZ * TOK, HEAD), BF16)

    forward(cache_ring, 1)
    begin_block()
    own(cache_ring, c_recv, 0)
    own(cache_ring, c_recv, 1)
    prepare(0, z)
    next_queries(1)
    g0 = wait_queries(0)
    first(g0)
    arrive(cache_ring, 1)
    prepare_pair(1)
    pair(g0, 1)
    next_queries(2)
    g1 = wait_queries(1)
    first(g1)
    forward(cache_ring, 2)
    forward(block_ring, 1)
    pair(g1, 1)
    next_queries(3)
    g2 = wait_queries(2)
    first(g2)
    pair(g2, 1)
    arrive(cache_ring, 2)
    prepare_pair(2)
    forward(cache_ring, 3)
    pair(g0, 2)
    forward(block_ring, 2)
    pair(g1, 2)
    g3 = wait_queries(3)
    first(g3)
    pair(g3, 1)
    forward(cache_ring, 4)
    pair(g2, 2)
    forward(block_ring, 3)
    pair(g3, 2)
    arrive(cache_ring, 3)
    prepare_pair(3)
    own(block_ring, b_recv, 1 - c)
    pair(g0, 3)
    forward(block_ring, 4)
    for g in (g1, g2, g3):
        pair(g, 3)
    arrive(cache_ring, 4)
    prepare_pair(4)
    for s in (1, 2, 3, 4):
        arrive(block_ring, s)
    prepare_block()

    def finish(r, carry):
        g = (x + r + 1) % NX
        for n in range(NX):
            pl.when(g == n)(functools.partial(last, n))
        send_result(g)
        return carry

    lax.fori_loop(0, NX, finish, 0)

    for k in range(4):

        @pl.when(jnp.logical_not(to_self(k)))
        def _():
            cache_piece(k).wait_send()

        block_piece(k).wait_send()
        near_piece(k // 2, k % 2).wait_send()
    query_piece(3).wait_send()
    drain(cache_ring)
    drain(block_ring)
    for g in range(4):

        @pl.when(jnp.logical_not(keep(g)))
        def _():
            result_piece(g).wait_send()

    for p in range(4):
        piece = out.at[:, pl.ds(p * 1024, 1024)]
        remote(piece, piece, o_send.at[p], o_recv.at[p], sibling).wait_recv()


def body(
    q_mant,
    q_scale,
    key_mantissa_block,
    key_exponent_scale,
    value_mantissa_block,
    value_exponent_scale,
    cached_key_rows,
    cached_value_rows,
    start,
):
    vmem = pl.BlockSpec(memory_space=pltpu.VMEM)
    anywhere = pl.BlockSpec(memory_space=pl.ANY)
    dma = pltpu.SemaphoreType.DMA
    result = pl.pallas_call(
        kernel,
        out_shape=pltpu.VMEM((TOK, 4096), BF16),
        in_specs=[
            *[anywhere] * 8,
            pl.BlockSpec(memory_space=pltpu.SMEM),
        ],
        out_specs=vmem,
        scratch_shapes=[
            pltpu.VMEM((TOK, 4096), BF16),
            pltpu.VMEM((TOK, 128), jnp.int32),
            pltpu.VMEM((TOK, 256), BF16),
            pltpu.VMEM((8, TOK), jnp.int32),
            pltpu.VMEM((TOK, 256), BF16),
            pltpu.VMEM((8, TOK), jnp.int32),
            pltpu.VMEM((2, 2 * CROWS, HEAD), BF16),
            pltpu.VMEM((4, ROWS, HEAD), BF16),
            pltpu.VMEM((2, 2 * TOK, HEAD), BF16),
            pltpu.VMEM((NX, ROWS, HEAD), BF16),
            pltpu.VMEM((NZ, NX, 2 * CROWS, HEAD), BF16),
            pltpu.VMEM((NZ, NX, 2 * TOK, HEAD), BF16),
            pltpu.VMEM((NZ * NX * CROWS, HEAD), BF16),
            pltpu.VMEM((NZ * NX * CROWS, 2 * HEAD), BF16),
            pltpu.VMEM((NZ * NX * TOK, HEAD), BF16),
            pltpu.VMEM((NZ * NX * TOK, 2 * HEAD), BF16),
            pltpu.VMEM((NX, ROWS, 2 * HEAD), F32),
            pltpu.VMEM((NX, ROWS, HEAD), F32),
            pltpu.VMEM((TILE, NZ * TOK), F32),
            pltpu.VMEM((NX, TOK, 1024), BF16),
            dma((10,)),
        ]
        + [dma((4,))] * 2
        + [dma((2, 2))] * 2
        + [dma((4,))] * 6
        + [dma((5, 2))] * 8,
        compiler_params=pltpu.CompilerParams(
            collective_id=0, has_side_effects=True, vmem_limit_bytes=56 << 20
        ),
        name="attend",
    )(
        q_mant[0],
        q_scale[0],
        key_mantissa_block[0],
        jnp.swapaxes(key_exponent_scale[0], 0, 1),
        value_mantissa_block[0],
        jnp.swapaxes(value_exponent_scale[0], 0, 1),
        cached_key_rows[0],
        cached_value_rows[0],
        start,
    )
    return result[None]


def solution(mesh):
    return jax.shard_map(
        body,
        mesh=mesh,
        in_specs=(
            P("section", "seq", "tensor"),
            P("section", "seq", "tensor"),
            P("section", "seq", "tensor"),
            P("section", "seq", "tensor"),
            P("section", "seq", "tensor"),
            P("section", "seq", "tensor"),
            P("section", "tensor", "seq", None),
            P("section", "tensor", "seq", None),
            P("section"),
        ),
        out_specs=P("section", "seq", "tensor"),
        check_vma=False,
    )
```

```python
import functools
import math

import jax
import jax.numpy as jnp
from jax import lax
from jax.experimental import pallas as pl
from jax.experimental.pallas import tpu as pltpu
from jax.sharding import PartitionSpec as P

BF16, F32 = jnp.bfloat16, jnp.float32
MESH = pl.DeviceIdType.MESH
NX, NZ = 4, 8
HEAD = 128
GROUP_HEADS = 8
TOK = 64
CROWS = 128
ROWS = GROUP_HEADS * TOK
TILE = 128
CHUNK = NX * CROWS
SCALE = (1.0 / math.sqrt(HEAD)) * math.log2(math.e)
NEG = -1e30
PLAN = (
    "N B C Q0 Q1 Q2 Q3 c1 b o O a1 c2 k1 w0 f0 p01 a2 c3 k2 p02 w1 f1 p11 p12 c4 w2 f2 p21 p22 k3"
    " w3 f3 p31 p32 a3 p03 k4 p13 p23 p33 a4 e L"
)
NT = (((1,), (1,)), ((), ()))
TN = (((0,), (0,)), ((), ()))


def spread(first, blocks, features):
    row = lax.broadcasted_iota(jnp.int32, (blocks, features), 0)
    col = lax.broadcasted_iota(jnp.int32, (blocks, features), 1)
    return jnp.where(row == first + col // 32, 1.0, 0.0).astype(BF16)


def kernel(
    q_hbm,
    qs_hbm,
    km_hbm,
    ks_hbm,
    vm_hbm,
    vs_hbm,
    ck_hbm,
    cv_hbm,
    start,
    out,
    q_in,
    q_scale,
    k_mant,
    k_scale,
    v_mant,
    v_scale,
    stage,
    qst,
    bst,
    qbuf,
    cb,
    bb,
    kp,
    vp,
    kb,
    vb,
    acc,
    top,
    bias,
    ost,
    load_sem,
    c_send,
    c_recv,
    n_send,
    n_recv,
    b_send,
    b_recv,
    q_send,
    q_recv,
    o_send,
    o_recv,
    rc_send,
    rc_recv,
    sc_send,
    sc_recv,
    rb_send,
    rb_recv,
    sb_send,
    sb_recv,
):
    sec = lax.axis_index("section")
    seq = lax.axis_index("seq")
    ten = lax.axis_index("tensor")
    x, z = seq // NZ, seq % NZ
    yl, c = ten // 2, ten % 2
    other = 1 - sec

    def dev(s, xx, zz, cc):
        return {"section": s, "seq": xx * NZ + zz, "tensor": yl * 2 + cc}

    loads = []
    for i in range(2):
        loads.append((ck_hbm.at[i], stage.at[i, pl.ds(0, CROWS)]))
        loads.append((cv_hbm.at[i], stage.at[i, pl.ds(CROWS, CROWS)]))
    loads += [(q_hbm, q_in), (qs_hbm, q_scale), (km_hbm, k_mant), (ks_hbm, k_scale)]
    loads += [(vm_hbm, v_mant), (vs_hbm, v_scale)]
    loads = [pltpu.make_async_copy(a, b, load_sem.at[n]) for n, (a, b) in enumerate(loads)]
    for cp in loads:
        cp.start()

    def decode():
        power = jnp.exp2(q_scale[...].astype(F32))
        pick = spread(0, 32, 1024)
        for k in range(NX):
            factor = jnp.dot(
                power[:, k * 32 : (k + 1) * 32].astype(BF16), pick, preferred_element_type=F32
            )
            mant = q_in[:, pl.ds(k * 1024, 1024)].astype(F32)
            decoded = (mant * factor).astype(BF16)
            for h in range(GROUP_HEADS):
                qst[k, pl.ds(h * TOK, TOK), :] = decoded[:, h * HEAD : (h + 1) * HEAD]
        pick = spread(0, 8, 256)
        for at, mant, scale in ((0, k_mant, k_scale), (TOK, v_mant, v_scale)):
            power = jnp.exp2(scale[...].astype(F32)).astype(BF16)
            factor = lax.dot_general(power, pick, TN, preferred_element_type=F32)
            decoded = (mant[...].astype(F32) * factor).astype(BF16)
            for i in range(2):
                bst[i, pl.ds(at, TOK), :] = decoded[:, i * HEAD : (i + 1) * HEAD]

    barrier = pltpu.get_barrier_semaphore()
    for ds in range(2):
        for dx in range(NX):
            for dc in range(2):
                if ds == 0 and dx == 0 and dc == 0:
                    continue
                pl.semaphore_signal(
                    barrier,
                    inc=1,
                    device_id=dev((sec + ds) % 2, (x + dx) % NX, z, (c + dc) % 2),
                    device_id_type=MESH,
                )
    for dz in (1, NZ - 1):
        zz = (z + dz) % NZ
        for to in (dev(sec, x, zz, c), dev(sec, 2 * c, zz, x // 2), dev(sec, 2 * c + 1, zz, x // 2)):
            pl.semaphore_signal(barrier, inc=1, device_id=to, device_id_type=MESH)
    for cp in loads:
        cp.wait()
    decode()
    pl.semaphore_wait(barrier, 21)

    sibling = dev(sec, x, z, 1 - c)

    def remote(src, dst, ssem, rsem, to):
        return pltpu.make_async_remote_copy(
            src_ref=src, dst_ref=dst, send_sem=ssem, recv_sem=rsem, device_id=to, device_id_type=MESH
        )

    sends, recvs = {}, {}

    def launch(key, copy):
        copy.start()
        sends[key] = copy
        recvs[key] = copy

    def received(key):
        recvs.pop(key).wait_recv()

    def cache_piece(i):
        return remote(
            stage.at[i], cb.at[0, x], c_send.at[i], c_recv.at[x % 2], dev(sec, 2 * c + i, z, x // 2)
        )

    def send_cache():
        for i in range(2):

            @pl.when(2 * c + i == x)
            def _():
                pltpu.make_async_copy(stage.at[i], cb.at[0, x], c_recv.at[x % 2]).start()

            @pl.when(2 * c + i != x)
            def _():
                cache_piece(i).start()

            here = cb.at[0, 2 * c + i]
            recvs["c", i] = remote(here, here, c_send.at[i], c_recv.at[i], sibling)

    def cache_sent():
        for i in range(2):

            @pl.when(2 * c + i != x)
            def _():
                cache_piece(i).wait_send()

    def send_near():
        for d in range(2):
            zz = (z + (1, NZ - 1)[d]) % NZ
            for i in range(2):
                sends["n", d, i] = remote(
                    stage.at[i],
                    cb.at[1 + d, x],
                    n_send.at[d, i],
                    n_recv.at[d, x % 2],
                    dev(sec, 2 * c + i, zz, x // 2),
                )
                sends["n", d, i].start()
                here = cb.at[1 + d, 2 * c + i]
                recvs["n", d, i] = remote(here, here, n_send.at[d, i], n_recv.at[d, i], sibling)

    def query_piece(r):
        k = (x + r) % NX
        return remote(
            qst.at[k], qbuf.at[x], q_send.at[r], q_recv.at[x], dev(other, 2 * c + k // 2, z, k % 2)
        )

    def send_queries(r):
        sends["q", r] = query_piece(r)
        sends["q", r].start()
        g = (2 * (x % 2) + c - r + NX) % NX
        recvs["q", r] = remote(qbuf.at[g], qbuf.at[g], q_send.at[r], q_recv.at[g], sibling)

    def wait_queries(r):
        received(("q", r))
        return (2 * (x % 2) + c - r + NX) % NX


    def send_block():
        for i in range(2):
            sends["b", i] = remote(
                bst.at[i], bb.at[0, x], b_send.at[i], b_recv.at[x % 2], dev(other, 2 * c + i, z, x // 2)
            )
            sends["b", i].start()
            here = bb.at[0, 2 * c + i]
            recvs["b", i] = remote(here, here, b_send.at[i], b_recv.at[i], sibling)

    onward = (dev(sec, x, (z + 1) % NZ, c), dev(sec, x, (z + NZ - 1) % NZ, c))

    def slot(s, d):
        return 0 if s == 0 else (7 if s == 4 else 2 * s - 1 + d)

    def unit(buf, n, s, d, core):
        return buf.at[n, pl.ds(2 * core + d, 1) if s == 4 else pl.ds(2 * core, 2)]

    def hop(ring, s, d):
        buf, rs, rr = ring[:3]
        src, dst = unit(buf, slot(s - 1, d), s, d, c), unit(buf, slot(s, d), s, d, c)
        return remote(src, dst, rs.at[s, d], rr.at[s, d], onward[d])

    def across(ring, s, d):
        here = unit(ring[0], slot(s, d), s, d, c)
        return remote(here, here, ring[3].at[s, d], ring[4].at[s, d], sibling)

    def from_sibling(ring, s, d):
        here = unit(ring[0], slot(s, d), s, d, 1 - c)
        return remote(here, here, ring[3].at[s, d], ring[4].at[s, d], sibling)

    cache_ring = (cb, rc_send, rc_recv, sc_send, sc_recv)
    block_ring = (bb, rb_send, rb_recv, sb_send, sb_recv)

    def hops(ring, s):
        for d in range(2):
            launch(("hop", id(ring), s, d), hop(ring, s, d))

    def share(ring, s, d):
        copy = across(ring, s, d)
        copy.start()
        sends["across", id(ring), s, d] = copy
        recvs["across", id(ring), s, d] = from_sibling(ring, s, d)

    def begin_block():
        for i in range(2):
            received(("b", i))
        hops(block_ring, 1)
        share(block_ring, 0, 0)

    def begin_cache():
        for i in range(2):
            received(("c", i))
        share(cache_ring, 0, 0)

    def forward(ring, s):
        for d in range(2):
            if s == 1 and ring is cache_ring:
                for n in range(2):
                    received(("n", d, n))
            else:
                received(("hop", id(ring), s, d))
            if s < 4:
                launch(("hop", id(ring), s + 1, d), hop(ring, s + 1, d))
        for d in range(2):
            share(ring, s, d)

    def arrive(ring, s):
        for d in range(2 if s else 1):
            received(("across", id(ring), s, d))

    limit = start[0]

    def prepare(n, zz):
        for xx in range(NX):
            rows = pl.ds(n * NX * CROWS + xx * CROWS, CROWS)
            keys = cb[n, xx, pl.ds(0, CROWS), :]
            vals = cb[n, xx, pl.ds(CROWS, CROWS), :]
            ones = jnp.ones((CROWS, HEAD), BF16)
            if xx >= 2:
                at = xx * NZ * CROWS + zz * CROWS
                seen = at + lax.broadcasted_iota(jnp.int32, (CROWS, HEAD), 0) < limit
                keys = jnp.where(
                    seen, keys.astype(F32), cb[n, xx - 2, pl.ds(0, CROWS), :].astype(F32)
                ).astype(BF16)
                vals = jnp.where(seen, vals.astype(F32), 0.0).astype(BF16)
                ones = jnp.where(seen, 1.0, 0.0).astype(BF16)
            kp[rows, :] = keys
            vp[rows, pl.ds(0, HEAD)] = vals
            vp[rows, pl.ds(HEAD, HEAD)] = ones

    def prepare_pair(s):
        if s == 4:
            prepare(7, (z + 4) % NZ)
        else:
            prepare(2 * s - 1, (z - s + NZ) % NZ)
            prepare(2 * s, (z + s) % NZ)

    def prepare_block():
        for n in range(NZ):
            s = (n + 1) // 2
            zz = z if n == 0 else ((z + s) % NZ if n in (2, 4, 6, 7) else (z - s + NZ) % NZ)
            for xx in range(NX):
                rows = pl.ds(pl.multiple_of(xx * NZ * TOK + zz * TOK, TOK), TOK)
                kb[rows, :] = bb[n, xx, pl.ds(0, TOK), :]
                vb[rows, pl.ds(0, HEAD)] = bb[n, xx, pl.ds(TOK, TOK), :]

    def scores(g, t, keys):
        queries = qbuf[g, pl.ds(t * TILE, TILE), :]
        return lax.dot_general(queries, keys, NT, preferred_element_type=F32) * SCALE

    tiles = range(ROWS // TILE)

    def wide(a, width):
        return jnp.tile(a, (1, width // HEAD))

    def first(g):
        keys = pl.ds(0, CHUNK)
        raw = [scores(g, t, kp[keys, :]) for t in tiles]
        for t in tiles:
            rows = pl.ds(t * TILE, TILE)
            high = jnp.broadcast_to(jnp.max(raw[t], axis=1, keepdims=True), (TILE, HEAD))
            weights = jnp.exp2(raw[t] - wide(high, CHUNK)).astype(BF16)
            acc[g, rows, :] = jnp.dot(weights, vp[keys, :], preferred_element_type=F32)
            top[g, rows, :] = high

    def update(g, t, parts, values):
        rows = pl.ds(t * TILE, TILE)
        peak = jnp.max(parts[0], axis=1, keepdims=True)
        for part in parts[1:]:
            peak = jnp.maximum(peak, jnp.max(part, axis=1, keepdims=True))
        old = top[g, rows, :]
        high = jnp.maximum(old, jnp.broadcast_to(peak, (TILE, HEAD)))
        total = acc[g, rows, :] * wide(jnp.exp2(old - high), 2 * HEAD)
        for part, ref in zip(parts, values):
            weights = jnp.exp2(part - wide(high, part.shape[1])).astype(BF16)
            total = total + jnp.dot(weights, ref[...], preferred_element_type=F32)
        return high, total

    def pair(g, s):
        keys = pl.ds((2 * s - 1) * CHUNK, 2 * CHUNK)
        raw = [[scores(g, t, kp[keys, :])] for t in tiles]
        for t in tiles:
            rows = pl.ds(t * TILE, TILE)
            high, total = update(g, t, raw[t], [vp.at[keys]])
            acc[g, rows, :] = total
            top[g, rows, :] = high

    def last(g):
        far = pl.ds(7 * CHUNK, CHUNK)
        whole = pl.ds(0, g * NZ * TOK)
        diagonal = pl.ds(g * NZ * TOK, NZ * TOK)
        raw = []
        for t in tiles:
            parts = [scores(g, t, kp[far, :])]
            if g:
                parts.append(scores(g, t, kb[whole, :]))
            parts.append(scores(g, t, kb[diagonal, :]) + bias[...])
            raw.append(parts)
        values = [vp.at[far]] + ([vb.at[whole]] if g else []) + [vb.at[diagonal]]
        for t in tiles:
            high, total = update(g, t, raw[t], values)
            done = (total[:, :HEAD] / total[:, HEAD:]).astype(BF16)
            for j in range(TILE // TOK):
                h = t * (TILE // TOK) + j
                ost[g, :, pl.ds(h * HEAD, HEAD)] = done[j * TOK : (j + 1) * TOK, :]

    def result_piece(g):
        p = 2 * (x % 2) + c
        return remote(
            ost.at[g],
            out.at[:, pl.ds(pl.multiple_of(p * 1024, 1024), 1024)],
            o_send.at[g],
            o_recv.at[p],
            dev(sec, g, z, x // 2),
        )

    def keep(g):
        return jnp.logical_and(g == x, x // 2 == c)

    def send_result(g):
        @pl.when(keep(g))
        def _():
            p = 2 * (x % 2) + c
            pltpu.make_async_copy(
                ost.at[g], out.at[:, pl.ds(pl.multiple_of(p * 1024, 1024), 1024)], o_recv.at[p]
            ).start()

        @pl.when(jnp.logical_not(keep(g)))
        def _():
            result_piece(g).start()

    row = lax.broadcasted_iota(jnp.int32, (TILE, NZ * TOK), 0) % TOK
    col = lax.broadcasted_iota(jnp.int32, (TILE, NZ * TOK), 1)
    bias[...] = jnp.where(col <= z * TOK + row, 0.0, NEG)
    vb[:, pl.ds(HEAD, HEAD)] = jnp.ones((NX * NZ * TOK, HEAD), BF16)

    groups = [None] * NX

    def step(name):
        op, at = name[0], [int(a) for a in name[1:]]
        if op == "C":
            send_cache()
        elif op == "N":
            send_near()
        elif op == "Q":
            send_queries(at[0])
        elif op == "G":
            sends.pop(("q", at[0])).wait_send()
        elif op == "B":
            send_block()
        elif op == "b":
            begin_block()
        elif op == "o":
            begin_cache()
        elif op == "O":
            arrive(cache_ring, 0)
            prepare(0, z)
        elif op == "c":
            forward(cache_ring, at[0])
        elif op == "k":
            forward(block_ring, at[0])
        elif op == "a":
            arrive(cache_ring, at[0])
            prepare_pair(at[0])
        elif op == "e":
            for s in range(5):
                arrive(block_ring, s)
            prepare_block()
        elif op == "w":
            groups[at[0]] = wait_queries(at[0])
        elif op == "f":
            first(groups[at[0]])
        elif op == "p":
            pair(groups[at[0]], at[1])
        elif op == "L":
            lax.fori_loop(0, NX, finish, 0)

    def finish(r, carry):
        g = (x + r + 1) % NX
        for n in range(NX):
            pl.when(g == n)(functools.partial(last, n))
        send_result(g)
        return carry

    for name in PLAN.split():
        step(name)

    cache_sent()
    for copy in sends.values():
        copy.wait_send()
    for g in range(NX):

        @pl.when(jnp.logical_not(keep(g)))
        def _():
            result_piece(g).wait_send()

    for p in range(4):
        piece = out.at[:, pl.ds(p * 1024, 1024)]
        remote(piece, piece, o_send.at[p], o_recv.at[p], sibling).wait_recv()


def body(
    q_mant,
    q_scale,
    key_mantissa_block,
    key_exponent_scale,
    value_mantissa_block,
    value_exponent_scale,
    cached_key_rows,
    cached_value_rows,
    start,
):
    vmem = pl.BlockSpec(memory_space=pltpu.VMEM)
    anywhere = pl.BlockSpec(memory_space=pl.ANY)
    dma = pltpu.SemaphoreType.DMA
    result = pl.pallas_call(
        kernel,
        out_shape=pltpu.VMEM((TOK, 4096), BF16),
        in_specs=[
            *[anywhere] * 8,
            pl.BlockSpec(memory_space=pltpu.SMEM),
        ],
        out_specs=vmem,
        scratch_shapes=[
            pltpu.VMEM((TOK, 4096), BF16),
            pltpu.VMEM((TOK, 128), jnp.int32),
            pltpu.VMEM((TOK, 256), BF16),
            pltpu.VMEM((8, TOK), jnp.int32),
            pltpu.VMEM((TOK, 256), BF16),
            pltpu.VMEM((8, TOK), jnp.int32),
            pltpu.VMEM((2, 2 * CROWS, HEAD), BF16),
            pltpu.VMEM((4, ROWS, HEAD), BF16),
            pltpu.VMEM((2, 2 * TOK, HEAD), BF16),
            pltpu.VMEM((NX, ROWS, HEAD), BF16),
            pltpu.VMEM((NZ, NX, 2 * CROWS, HEAD), BF16),
            pltpu.VMEM((NZ, NX, 2 * TOK, HEAD), BF16),
            pltpu.VMEM((NZ * NX * CROWS, HEAD), BF16),
            pltpu.VMEM((NZ * NX * CROWS, 2 * HEAD), BF16),
            pltpu.VMEM((NZ * NX * TOK, HEAD), BF16),
            pltpu.VMEM((NZ * NX * TOK, 2 * HEAD), BF16),
            pltpu.VMEM((NX, ROWS, 2 * HEAD), F32),
            pltpu.VMEM((NX, ROWS, HEAD), F32),
            pltpu.VMEM((TILE, NZ * TOK), F32),
            pltpu.VMEM((NX, TOK, 1024), BF16),
            dma((10,)),
        ]
        + [dma((2,))] * 2
        + [dma((2, 2))] * 2
        + [dma((2,))] * 2
        + [dma((4,))] * 4
        + [dma((5, 2))] * 8,
        compiler_params=pltpu.CompilerParams(
            collective_id=0, has_side_effects=True, vmem_limit_bytes=56 << 20
        ),
        name="attend",
    )(
        q_mant[0],
        q_scale[0],
        key_mantissa_block[0],
        jnp.swapaxes(key_exponent_scale[0], 0, 1),
        value_mantissa_block[0],
        jnp.swapaxes(value_exponent_scale[0], 0, 1),
        cached_key_rows[0],
        cached_value_rows[0],
        start,
    )
    return result[None]


def solution(mesh):
    return jax.shard_map(
        body,
        mesh=mesh,
        in_specs=(
            P("section", "seq", "tensor"),
            P("section", "seq", "tensor"),
            P("section", "seq", "tensor"),
            P("section", "seq", "tensor"),
            P("section", "seq", "tensor"),
            P("section", "seq", "tensor"),
            P("section", "tensor", "seq", None),
            P("section", "tensor", "seq", None),
            P("section"),
        ),
        out_specs=P("section", "seq", "tensor"),
        check_vma=False,
    )
```

```python
import functools
import math

import jax
import jax.numpy as jnp
from jax import lax
from jax.experimental import pallas as pl
from jax.experimental.pallas import tpu as pltpu
from jax.sharding import PartitionSpec as P

BF16, F32 = jnp.bfloat16, jnp.float32
MESH = pl.DeviceIdType.MESH
NX, NZ = 4, 8
HEAD = 128
GROUP_HEADS = 8
TOK = 64
CROWS = 128
ROWS = GROUP_HEADS * TOK
TILE = 128
CHUNK = NX * CROWS
SCALE = (1.0 / math.sqrt(HEAD)) * math.log2(math.e)
NEG = -1e30
PLAN = (
    *("N B C Q0", "Q1 Q2 Q3", "c1 b o O", "a1 c2 k1", "w0 f0 p01", "a2 c3 k2", "p02 w1 f1", "p11 p12 c4"),
    *("w2 f2 p21", "p22 k3 w3", "f3 p31 p32", "a3 p03 k4", "p13 p23 p33", "e m3 m2", "m1 m0 a4", "L2 L1 L3 L0"),
)
NT = (((1,), (1,)), ((), ()))
TN = (((0,), (0,)), ((), ()))


def spread(first, blocks, features):
    row = lax.broadcasted_iota(jnp.int32, (blocks, features), 0)
    col = lax.broadcasted_iota(jnp.int32, (blocks, features), 1)
    return jnp.where(row == first + col // 32, 1.0, 0.0).astype(BF16)


def kernel(
    q_hbm,
    qs_hbm,
    km_hbm,
    ks_hbm,
    vm_hbm,
    vs_hbm,
    ck_hbm,
    cv_hbm,
    start,
    out,
    q_in,
    q_scale,
    k_mant,
    k_scale,
    v_mant,
    v_scale,
    stage,
    qst,
    bst,
    qbuf,
    cb,
    bb,
    kp,
    vp,
    kb,
    vb,
    acc,
    top,
    bias,
    ost,
    load_sem,
    c_send,
    c_recv,
    n_send,
    n_recv,
    b_send,
    b_recv,
    q_send,
    q_recv,
    o_send,
    o_recv,
    rc_send,
    rc_recv,
    sc_send,
    sc_recv,
    rb_send,
    rb_recv,
    sb_send,
    sb_recv,
):
    sec = lax.axis_index("section")
    seq = lax.axis_index("seq")
    ten = lax.axis_index("tensor")
    x, z = seq // NZ, seq % NZ
    yl, c = ten // 2, ten % 2
    other = 1 - sec

    def dev(s, xx, zz, cc):
        return {"section": s, "seq": xx * NZ + zz, "tensor": yl * 2 + cc}

    loads = []
    for i in range(2):
        loads.append((ck_hbm.at[i], stage.at[i, pl.ds(0, CROWS)]))
        loads.append((cv_hbm.at[i], stage.at[i, pl.ds(CROWS, CROWS)]))
    loads += [(q_hbm, q_in), (qs_hbm, q_scale), (km_hbm, k_mant), (ks_hbm, k_scale)]
    loads += [(vm_hbm, v_mant), (vs_hbm, v_scale)]
    loads = [pltpu.make_async_copy(a, b, load_sem.at[n]) for n, (a, b) in enumerate(loads)]
    for cp in loads:
        cp.start()

    def decode():
        power = jnp.exp2(q_scale[...].astype(F32))
        pick = spread(0, 32, 1024)
        for k in range(NX):
            factor = jnp.dot(
                power[:, k * 32 : (k + 1) * 32].astype(BF16), pick, preferred_element_type=F32
            )
            mant = q_in[:, pl.ds(k * 1024, 1024)].astype(F32)
            decoded = (mant * factor).astype(BF16)
            for h in range(GROUP_HEADS):
                qst[k, pl.ds(h * TOK, TOK), :] = decoded[:, h * HEAD : (h + 1) * HEAD]
        pick = spread(0, 8, 256)
        for at, mant, scale in ((0, k_mant, k_scale), (TOK, v_mant, v_scale)):
            power = jnp.exp2(scale[...].astype(F32)).astype(BF16)
            factor = lax.dot_general(power, pick, TN, preferred_element_type=F32)
            decoded = (mant[...].astype(F32) * factor).astype(BF16)
            for i in range(2):
                bst[i, pl.ds(at, TOK), :] = decoded[:, i * HEAD : (i + 1) * HEAD]

    barrier = pltpu.get_barrier_semaphore()
    for ds in range(2):
        for dx in range(NX):
            for dc in range(2):
                if ds == 0 and dx == 0 and dc == 0:
                    continue
                pl.semaphore_signal(
                    barrier,
                    inc=1,
                    device_id=dev((sec + ds) % 2, (x + dx) % NX, z, (c + dc) % 2),
                    device_id_type=MESH,
                )
    for dz in (1, NZ - 1):
        zz = (z + dz) % NZ
        for to in (dev(sec, x, zz, c), dev(sec, 2 * c, zz, x // 2), dev(sec, 2 * c + 1, zz, x // 2)):
            pl.semaphore_signal(barrier, inc=1, device_id=to, device_id_type=MESH)
    for cp in loads:
        cp.wait()
    decode()
    pl.semaphore_wait(barrier, 21)

    sibling = dev(sec, x, z, 1 - c)

    def remote(src, dst, ssem, rsem, to):
        return pltpu.make_async_remote_copy(
            src_ref=src, dst_ref=dst, send_sem=ssem, recv_sem=rsem, device_id=to, device_id_type=MESH
        )

    sends, recvs = {}, {}

    def launch(key, copy):
        copy.start()
        sends[key] = copy
        recvs[key] = copy

    def received(key):
        recvs.pop(key).wait_recv()

    def cache_piece(i):
        return remote(
            stage.at[i], cb.at[0, x], c_send.at[i], c_recv.at[x % 2], dev(sec, 2 * c + i, z, x // 2)
        )

    def send_cache():
        for i in range(2):

            @pl.when(2 * c + i == x)
            def _():
                pltpu.make_async_copy(stage.at[i], cb.at[0, x], c_recv.at[x % 2]).start()

            @pl.when(2 * c + i != x)
            def _():
                cache_piece(i).start()

            here = cb.at[0, 2 * c + i]
            recvs["c", i] = remote(here, here, c_send.at[i], c_recv.at[i], sibling)

    def cache_sent():
        for i in range(2):

            @pl.when(2 * c + i != x)
            def _():
                cache_piece(i).wait_send()

    def send_near():
        for d in range(2):
            zz = (z + (1, NZ - 1)[d]) % NZ
            for i in range(2):
                sends["n", d, i] = remote(
                    stage.at[i],
                    cb.at[1 + d, x],
                    n_send.at[d, i],
                    n_recv.at[d, x % 2],
                    dev(sec, 2 * c + i, zz, x // 2),
                )
                sends["n", d, i].start()
                here = cb.at[1 + d, 2 * c + i]
                recvs["n", d, i] = remote(here, here, n_send.at[d, i], n_recv.at[d, i], sibling)

    def query_piece(r):
        k = (x + r) % NX
        return remote(
            qst.at[k], qbuf.at[x], q_send.at[r], q_recv.at[x], dev(other, 2 * c + k // 2, z, k % 2)
        )

    def send_queries(r):
        sends["q", r] = query_piece(r)
        sends["q", r].start()
        g = (2 * (x % 2) + c - r + NX) % NX
        recvs["q", r] = remote(qbuf.at[g], qbuf.at[g], q_send.at[r], q_recv.at[g], sibling)

    def wait_queries(r):
        received(("q", r))
        return (2 * (x % 2) + c - r + NX) % NX


    def send_block():
        for i in range(2):
            sends["b", i] = remote(
                bst.at[i], bb.at[0, x], b_send.at[i], b_recv.at[x % 2], dev(other, 2 * c + i, z, x // 2)
            )
            sends["b", i].start()
            here = bb.at[0, 2 * c + i]
            recvs["b", i] = remote(here, here, b_send.at[i], b_recv.at[i], sibling)

    onward = (dev(sec, x, (z + 1) % NZ, c), dev(sec, x, (z + NZ - 1) % NZ, c))

    def slot(s, d):
        return 0 if s == 0 else (7 if s == 4 else 2 * s - 1 + d)

    def unit(buf, n, s, d, core):
        return buf.at[n, pl.ds(2 * core + d, 1) if s == 4 else pl.ds(2 * core, 2)]

    def hop(ring, s, d):
        buf, rs, rr = ring[:3]
        src, dst = unit(buf, slot(s - 1, d), s, d, c), unit(buf, slot(s, d), s, d, c)
        return remote(src, dst, rs.at[s, d], rr.at[s, d], onward[d])

    def across(ring, s, d):
        here = unit(ring[0], slot(s, d), s, d, c)
        return remote(here, here, ring[3].at[s, d], ring[4].at[s, d], sibling)

    def from_sibling(ring, s, d):
        here = unit(ring[0], slot(s, d), s, d, 1 - c)
        return remote(here, here, ring[3].at[s, d], ring[4].at[s, d], sibling)

    cache_ring = (cb, rc_send, rc_recv, sc_send, sc_recv)
    block_ring = (bb, rb_send, rb_recv, sb_send, sb_recv)

    def hops(ring, s):
        for d in range(2):
            launch(("hop", id(ring), s, d), hop(ring, s, d))

    def share(ring, s, d):
        copy = across(ring, s, d)
        copy.start()
        sends["across", id(ring), s, d] = copy
        recvs["across", id(ring), s, d] = from_sibling(ring, s, d)

    def begin_block():
        for i in range(2):
            received(("b", i))
        hops(block_ring, 1)
        share(block_ring, 0, 0)

    def begin_cache():
        for i in range(2):
            received(("c", i))
        share(cache_ring, 0, 0)

    def forward(ring, s):
        for d in range(2):
            if s == 1 and ring is cache_ring:
                for n in range(2):
                    received(("n", d, n))
            else:
                received(("hop", id(ring), s, d))
            if s < 4:
                launch(("hop", id(ring), s + 1, d), hop(ring, s + 1, d))
        for d in range(2):
            share(ring, s, d)

    def arrive(ring, s):
        for d in range(2 if s else 1):
            received(("across", id(ring), s, d))

    limit = start[0]

    def prepare(n, zz):
        for xx in range(NX):
            rows = pl.ds(n * NX * CROWS + xx * CROWS, CROWS)
            keys = cb[n, xx, pl.ds(0, CROWS), :]
            vals = cb[n, xx, pl.ds(CROWS, CROWS), :]
            ones = jnp.ones((CROWS, HEAD), BF16)
            if xx >= 2:
                at = xx * NZ * CROWS + zz * CROWS
                seen = at + lax.broadcasted_iota(jnp.int32, (CROWS, HEAD), 0) < limit
                keys = jnp.where(
                    seen, keys.astype(F32), cb[n, xx - 2, pl.ds(0, CROWS), :].astype(F32)
                ).astype(BF16)
                vals = jnp.where(seen, vals.astype(F32), 0.0).astype(BF16)
                ones = jnp.where(seen, 1.0, 0.0).astype(BF16)
            kp[rows, :] = keys
            vp[rows, pl.ds(0, HEAD)] = vals
            vp[rows, pl.ds(HEAD, HEAD)] = ones

    def prepare_pair(s):
        if s == 4:
            prepare(7, (z + 4) % NZ)
        else:
            prepare(2 * s - 1, (z - s + NZ) % NZ)
            prepare(2 * s, (z + s) % NZ)

    def prepare_block():
        for n in range(NZ):
            s = (n + 1) // 2
            zz = z if n == 0 else ((z + s) % NZ if n in (2, 4, 6, 7) else (z - s + NZ) % NZ)
            for xx in range(NX):
                rows = pl.ds(pl.multiple_of(xx * NZ * TOK + zz * TOK, TOK), TOK)
                kb[rows, :] = bb[n, xx, pl.ds(0, TOK), :]
                vb[rows, pl.ds(0, HEAD)] = bb[n, xx, pl.ds(TOK, TOK), :]

    def scores(g, t, keys):
        queries = qbuf[g, pl.ds(t * TILE, TILE), :]
        return lax.dot_general(queries, keys, NT, preferred_element_type=F32) * SCALE

    tiles = range(ROWS // TILE)

    def wide(a, width):
        return jnp.tile(a, (1, width // HEAD))

    def first(g):
        keys = pl.ds(0, CHUNK)
        raw = [scores(g, t, kp[keys, :]) for t in tiles]
        for t in tiles:
            rows = pl.ds(t * TILE, TILE)
            high = jnp.broadcast_to(jnp.max(raw[t], axis=1, keepdims=True), (TILE, HEAD))
            weights = jnp.exp2(raw[t] - wide(high, CHUNK)).astype(BF16)
            acc[g, rows, :] = jnp.dot(weights, vp[keys, :], preferred_element_type=F32)
            top[g, rows, :] = high

    def update(g, t, parts, values):
        rows = pl.ds(t * TILE, TILE)
        peak = jnp.max(parts[0], axis=1, keepdims=True)
        for part in parts[1:]:
            peak = jnp.maximum(peak, jnp.max(part, axis=1, keepdims=True))
        old = top[g, rows, :]
        high = jnp.maximum(old, jnp.broadcast_to(peak, (TILE, HEAD)))
        total = acc[g, rows, :] * wide(jnp.exp2(old - high), 2 * HEAD)
        for part, ref in zip(parts, values):
            weights = jnp.exp2(part - wide(high, part.shape[1])).astype(BF16)
            total = total + jnp.dot(weights, ref[...], preferred_element_type=F32)
        return high, total

    def pair(g, s):
        keys = pl.ds((2 * s - 1) * CHUNK, 2 * CHUNK)
        raw = [[scores(g, t, kp[keys, :])] for t in tiles]
        for t in tiles:
            rows = pl.ds(t * TILE, TILE)
            high, total = update(g, t, raw[t], [vp.at[keys]])
            acc[g, rows, :] = total
            top[g, rows, :] = high

    def block(g):
        whole = pl.ds(0, g * NZ * TOK)
        diagonal = pl.ds(g * NZ * TOK, NZ * TOK)
        raw = []
        for t in tiles:
            parts = [scores(g, t, kb[whole, :])] if g else []
            raw.append(parts + [scores(g, t, kb[diagonal, :]) + bias[...]])
        values = ([vb.at[whole]] if g else []) + [vb.at[diagonal]]
        for t in tiles:
            rows = pl.ds(t * TILE, TILE)
            high, total = update(g, t, raw[t], values)
            acc[g, rows, :] = total
            top[g, rows, :] = high

    def last(g):
        far = pl.ds(7 * CHUNK, CHUNK)
        raw = [[scores(g, t, kp[far, :])] for t in tiles]
        for t in tiles:
            high, total = update(g, t, raw[t], [vp.at[far]])
            done = (total[:, :HEAD] / total[:, HEAD:]).astype(BF16)
            for j in range(TILE // TOK):
                h = t * (TILE // TOK) + j
                ost[g, :, pl.ds(h * HEAD, HEAD)] = done[j * TOK : (j + 1) * TOK, :]

    def result_piece(g):
        p = 2 * (x % 2) + c
        return remote(
            ost.at[g],
            out.at[:, pl.ds(pl.multiple_of(p * 1024, 1024), 1024)],
            o_send.at[g],
            o_recv.at[p],
            dev(sec, g, z, x // 2),
        )

    def keep(g):
        return jnp.logical_and(g == x, x // 2 == c)

    def send_result(g):
        @pl.when(keep(g))
        def _():
            p = 2 * (x % 2) + c
            pltpu.make_async_copy(
                ost.at[g], out.at[:, pl.ds(pl.multiple_of(p * 1024, 1024), 1024)], o_recv.at[p]
            ).start()

        @pl.when(jnp.logical_not(keep(g)))
        def _():
            result_piece(g).start()

    row = lax.broadcasted_iota(jnp.int32, (TILE, NZ * TOK), 0) % TOK
    col = lax.broadcasted_iota(jnp.int32, (TILE, NZ * TOK), 1)
    bias[...] = jnp.where(col <= z * TOK + row, 0.0, NEG)
    vb[:, pl.ds(HEAD, HEAD)] = jnp.ones((NX * NZ * TOK, HEAD), BF16)

    groups = [None] * NX

    def step(name):
        op, at = name[0], [int(a) for a in name[1:]]
        if op == "C":
            send_cache()
        elif op == "N":
            send_near()
        elif op == "Q":
            send_queries(at[0])
        elif op == "G":
            sends.pop(("q", at[0])).wait_send()
        elif op == "B":
            send_block()
        elif op == "b":
            begin_block()
        elif op == "o":
            begin_cache()
        elif op == "O":
            arrive(cache_ring, 0)
            prepare(0, z)
        elif op == "c":
            forward(cache_ring, at[0])
        elif op == "k":
            forward(block_ring, at[0])
        elif op == "a":
            arrive(cache_ring, at[0])
            prepare_pair(at[0])
        elif op == "e":
            for s in range(5):
                arrive(block_ring, s)
            prepare_block()
        elif op == "w":
            groups[at[0]] = wait_queries(at[0])
        elif op == "f":
            first(groups[at[0]])
        elif op == "p":
            pair(groups[at[0]], at[1])
        elif op == "m":
            block(at[0])
        elif op == "L":
            g = (x + at[0]) % NX
            last(g)
            send_result(g)

    for names in PLAN:
        for name in names.split():
            step(name)

    cache_sent()
    for copy in sends.values():
        copy.wait_send()
    for g in range(NX):

        @pl.when(jnp.logical_not(keep(g)))
        def _():
            result_piece(g).wait_send()

    for p in range(4):
        piece = out.at[:, pl.ds(p * 1024, 1024)]
        remote(piece, piece, o_send.at[p], o_recv.at[p], sibling).wait_recv()


def body(
    q_mant,
    q_scale,
    key_mantissa_block,
    key_exponent_scale,
    value_mantissa_block,
    value_exponent_scale,
    cached_key_rows,
    cached_value_rows,
    start,
):
    vmem = pl.BlockSpec(memory_space=pltpu.VMEM)
    anywhere = pl.BlockSpec(memory_space=pl.ANY)
    dma = pltpu.SemaphoreType.DMA
    result = pl.pallas_call(
        kernel,
        out_shape=pltpu.VMEM((TOK, 4096), BF16),
        in_specs=[
            *[anywhere] * 8,
            pl.BlockSpec(memory_space=pltpu.SMEM),
        ],
        out_specs=vmem,
        scratch_shapes=[
            pltpu.VMEM((TOK, 4096), BF16),
            pltpu.VMEM((TOK, 128), jnp.int32),
            pltpu.VMEM((TOK, 256), BF16),
            pltpu.VMEM((8, TOK), jnp.int32),
            pltpu.VMEM((TOK, 256), BF16),
            pltpu.VMEM((8, TOK), jnp.int32),
            pltpu.VMEM((2, 2 * CROWS, HEAD), BF16),
            pltpu.VMEM((4, ROWS, HEAD), BF16),
            pltpu.VMEM((2, 2 * TOK, HEAD), BF16),
            pltpu.VMEM((NX, ROWS, HEAD), BF16),
            pltpu.VMEM((NZ, NX, 2 * CROWS, HEAD), BF16),
            pltpu.VMEM((NZ, NX, 2 * TOK, HEAD), BF16),
            pltpu.VMEM((NZ * NX * CROWS, HEAD), BF16),
            pltpu.VMEM((NZ * NX * CROWS, 2 * HEAD), BF16),
            pltpu.VMEM((NZ * NX * TOK, HEAD), BF16),
            pltpu.VMEM((NZ * NX * TOK, 2 * HEAD), BF16),
            pltpu.VMEM((NX, ROWS, 2 * HEAD), F32),
            pltpu.VMEM((NX, ROWS, HEAD), F32),
            pltpu.VMEM((TILE, NZ * TOK), F32),
            pltpu.VMEM((NX, TOK, 1024), BF16),
            dma((10,)),
        ]
        + [dma((2,))] * 2
        + [dma((2, 2))] * 2
        + [dma((2,))] * 2
        + [dma((4,))] * 4
        + [dma((5, 2))] * 8,
        compiler_params=pltpu.CompilerParams(
            collective_id=0, has_side_effects=True, vmem_limit_bytes=56 << 20
        ),
        name="attend",
    )(
        q_mant[0],
        q_scale[0],
        key_mantissa_block[0],
        jnp.swapaxes(key_exponent_scale[0], 0, 1),
        value_mantissa_block[0],
        jnp.swapaxes(value_exponent_scale[0], 0, 1),
        cached_key_rows[0],
        cached_value_rows[0],
        start,
    )
    return result[None]


def solution(mesh):
    return jax.shard_map(
        body,
        mesh=mesh,
        in_specs=(
            P("section", "seq", "tensor"),
            P("section", "seq", "tensor"),
            P("section", "seq", "tensor"),
            P("section", "seq", "tensor"),
            P("section", "seq", "tensor"),
            P("section", "seq", "tensor"),
            P("section", "tensor", "seq", None),
            P("section", "tensor", "seq", None),
            P("section"),
        ),
        out_specs=P("section", "seq", "tensor"),
        check_vma=False,
    )
```

```python
import functools
import math

import jax
import jax.numpy as jnp
from jax import lax
from jax.experimental import pallas as pl
from jax.experimental.pallas import tpu as pltpu
from jax.sharding import PartitionSpec as P

BF16, F32 = jnp.bfloat16, jnp.float32
MESH = pl.DeviceIdType.MESH
NX, NZ = 4, 8
HEAD = 128
GROUP_HEADS = 8
TOK = 64
CROWS = 128
ROWS = GROUP_HEADS * TOK
TILE = 128
CHUNK = NX * CROWS
SCALE = (1.0 / math.sqrt(HEAD)) * math.log2(math.e)
NEG = -1e30
PLAN = (
    *("N B C Q0", "Q1 Q2 Q3", "c1 b o O", "a1 c2 k1", "w0 s002", "w1 s102", "a2 s034 c3 k2"),
    *("s134 w2 s204", "c4 k3 a3", "s056 s156", "w3 s306 k4", "s256 e a4 L"),
)
NT = (((1,), (1,)), ((), ()))
TN = (((0,), (0,)), ((), ()))


def spread(first, blocks, features):
    row = lax.broadcasted_iota(jnp.int32, (blocks, features), 0)
    col = lax.broadcasted_iota(jnp.int32, (blocks, features), 1)
    return jnp.where(row == first + col // 32, 1.0, 0.0).astype(BF16)


def kernel(
    q_hbm,
    qs_hbm,
    km_hbm,
    ks_hbm,
    vm_hbm,
    vs_hbm,
    ck_hbm,
    cv_hbm,
    start,
    out,
    q_in,
    q_scale,
    k_mant,
    k_scale,
    v_mant,
    v_scale,
    stage,
    qst,
    bst,
    qbuf,
    cb,
    bb,
    kp,
    vp,
    kb,
    vb,
    acc,
    top,
    bias,
    ost,
    load_sem,
    c_send,
    c_recv,
    n_send,
    n_recv,
    b_send,
    b_recv,
    q_send,
    q_recv,
    o_send,
    o_recv,
    rc_send,
    rc_recv,
    sc_send,
    sc_recv,
    rb_send,
    rb_recv,
    sb_send,
    sb_recv,
):
    sec = lax.axis_index("section")
    seq = lax.axis_index("seq")
    ten = lax.axis_index("tensor")
    x, z = seq // NZ, seq % NZ
    yl, c = ten // 2, ten % 2
    other = 1 - sec

    def dev(s, xx, zz, cc):
        return {"section": s, "seq": xx * NZ + zz, "tensor": yl * 2 + cc}

    loads = []
    for i in range(2):
        loads.append((ck_hbm.at[i], stage.at[i, pl.ds(0, CROWS)]))
        loads.append((cv_hbm.at[i], stage.at[i, pl.ds(CROWS, CROWS)]))
    loads += [(q_hbm, q_in), (qs_hbm, q_scale), (km_hbm, k_mant), (ks_hbm, k_scale)]
    loads += [(vm_hbm, v_mant), (vs_hbm, v_scale)]
    loads = [pltpu.make_async_copy(a, b, load_sem.at[n]) for n, (a, b) in enumerate(loads)]
    for cp in loads:
        cp.start()

    def decode():
        power = jnp.exp2(q_scale[...].astype(F32))
        pick = spread(0, 32, 1024)
        for k in range(NX):
            factor = jnp.dot(
                power[:, k * 32 : (k + 1) * 32].astype(BF16), pick, preferred_element_type=F32
            )
            mant = q_in[:, pl.ds(k * 1024, 1024)].astype(F32)
            decoded = (mant * factor).astype(BF16)
            for h in range(GROUP_HEADS):
                qst[k, pl.ds(h * TOK, TOK), :] = decoded[:, h * HEAD : (h + 1) * HEAD]
        pick = spread(0, 8, 256)
        for at, mant, scale in ((0, k_mant, k_scale), (TOK, v_mant, v_scale)):
            power = jnp.exp2(scale[...].astype(F32)).astype(BF16)
            factor = lax.dot_general(power, pick, TN, preferred_element_type=F32)
            decoded = (mant[...].astype(F32) * factor).astype(BF16)
            for i in range(2):
                bst[i, pl.ds(at, TOK), :] = decoded[:, i * HEAD : (i + 1) * HEAD]

    barrier = pltpu.get_barrier_semaphore()
    for ds in range(2):
        for dx in range(NX):
            for dc in range(2):
                if ds == 0 and dx == 0 and dc == 0:
                    continue
                pl.semaphore_signal(
                    barrier,
                    inc=1,
                    device_id=dev((sec + ds) % 2, (x + dx) % NX, z, (c + dc) % 2),
                    device_id_type=MESH,
                )
    for dz in (1, NZ - 1):
        zz = (z + dz) % NZ
        for to in (dev(sec, x, zz, c), dev(sec, 2 * c, zz, x // 2), dev(sec, 2 * c + 1, zz, x // 2)):
            pl.semaphore_signal(barrier, inc=1, device_id=to, device_id_type=MESH)
    for cp in loads:
        cp.wait()
    decode()
    pl.semaphore_wait(barrier, 21)

    sibling = dev(sec, x, z, 1 - c)

    def remote(src, dst, ssem, rsem, to):
        return pltpu.make_async_remote_copy(
            src_ref=src, dst_ref=dst, send_sem=ssem, recv_sem=rsem, device_id=to, device_id_type=MESH
        )

    sends, recvs = {}, {}

    def launch(key, copy):
        copy.start()
        sends[key] = copy
        recvs[key] = copy

    def received(key):
        recvs.pop(key).wait_recv()

    def cache_piece(i):
        return remote(
            stage.at[i], cb.at[0, x], c_send.at[i], c_recv.at[x % 2], dev(sec, 2 * c + i, z, x // 2)
        )

    def send_cache():
        for i in range(2):

            @pl.when(2 * c + i == x)
            def _():
                pltpu.make_async_copy(stage.at[i], cb.at[0, x], c_recv.at[x % 2]).start()

            @pl.when(2 * c + i != x)
            def _():
                cache_piece(i).start()

            here = cb.at[0, 2 * c + i]
            recvs["c", i] = remote(here, here, c_send.at[i], c_recv.at[i], sibling)

    def cache_sent():
        for i in range(2):

            @pl.when(2 * c + i != x)
            def _():
                cache_piece(i).wait_send()

    def send_near():
        for d in range(2):
            zz = (z + (1, NZ - 1)[d]) % NZ
            for i in range(2):
                sends["n", d, i] = remote(
                    stage.at[i],
                    cb.at[1 + d, x],
                    n_send.at[d, i],
                    n_recv.at[d, x % 2],
                    dev(sec, 2 * c + i, zz, x // 2),
                )
                sends["n", d, i].start()
                here = cb.at[1 + d, 2 * c + i]
                recvs["n", d, i] = remote(here, here, n_send.at[d, i], n_recv.at[d, i], sibling)

    def query_piece(r):
        k = (x + r) % NX
        return remote(
            qst.at[k], qbuf.at[x], q_send.at[r], q_recv.at[x], dev(other, 2 * c + k // 2, z, k % 2)
        )

    def send_queries(r):
        sends["q", r] = query_piece(r)
        sends["q", r].start()
        g = (2 * (x % 2) + c - r + NX) % NX
        recvs["q", r] = remote(qbuf.at[g], qbuf.at[g], q_send.at[r], q_recv.at[g], sibling)

    def wait_queries(r):
        received(("q", r))
        return (2 * (x % 2) + c - r + NX) % NX


    def send_block():
        for i in range(2):
            sends["b", i] = remote(
                bst.at[i], bb.at[0, x], b_send.at[i], b_recv.at[x % 2], dev(other, 2 * c + i, z, x // 2)
            )
            sends["b", i].start()
            here = bb.at[0, 2 * c + i]
            recvs["b", i] = remote(here, here, b_send.at[i], b_recv.at[i], sibling)

    onward = (dev(sec, x, (z + 1) % NZ, c), dev(sec, x, (z + NZ - 1) % NZ, c))

    def slot(s, d):
        return 0 if s == 0 else (7 if s == 4 else 2 * s - 1 + d)

    def unit(buf, n, s, d, core):
        return buf.at[n, pl.ds(2 * core + d, 1) if s == 4 else pl.ds(2 * core, 2)]

    def hop(ring, s, d):
        buf, rs, rr = ring[:3]
        src, dst = unit(buf, slot(s - 1, d), s, d, c), unit(buf, slot(s, d), s, d, c)
        return remote(src, dst, rs.at[s, d], rr.at[s, d], onward[d])

    def across(ring, s, d):
        here = unit(ring[0], slot(s, d), s, d, c)
        return remote(here, here, ring[3].at[s, d], ring[4].at[s, d], sibling)

    def from_sibling(ring, s, d):
        here = unit(ring[0], slot(s, d), s, d, 1 - c)
        return remote(here, here, ring[3].at[s, d], ring[4].at[s, d], sibling)

    cache_ring = (cb, rc_send, rc_recv, sc_send, sc_recv)
    block_ring = (bb, rb_send, rb_recv, sb_send, sb_recv)

    def hops(ring, s):
        for d in range(2):
            launch(("hop", id(ring), s, d), hop(ring, s, d))

    def share(ring, s, d):
        copy = across(ring, s, d)
        copy.start()
        sends["across", id(ring), s, d] = copy
        recvs["across", id(ring), s, d] = from_sibling(ring, s, d)

    def begin_block():
        for i in range(2):
            received(("b", i))
        hops(block_ring, 1)
        share(block_ring, 0, 0)

    def begin_cache():
        for i in range(2):
            received(("c", i))
        share(cache_ring, 0, 0)

    def forward(ring, s):
        for d in range(2):
            if s == 1 and ring is cache_ring:
                for n in range(2):
                    received(("n", d, n))
            else:
                received(("hop", id(ring), s, d))
            if s < 4:
                launch(("hop", id(ring), s + 1, d), hop(ring, s + 1, d))
        for d in range(2):
            share(ring, s, d)

    def arrive(ring, s):
        for d in range(2 if s else 1):
            received(("across", id(ring), s, d))

    limit = start[0]

    def prepare(n, zz):
        for xx in range(NX):
            rows = pl.ds(n * NX * CROWS + xx * CROWS, CROWS)
            keys = cb[n, xx, pl.ds(0, CROWS), :]
            vals = cb[n, xx, pl.ds(CROWS, CROWS), :]
            ones = jnp.ones((CROWS, HEAD), BF16)
            if xx >= 2:
                at = xx * NZ * CROWS + zz * CROWS
                seen = at + lax.broadcasted_iota(jnp.int32, (CROWS, HEAD), 0) < limit
                keys = jnp.where(
                    seen, keys.astype(F32), cb[n, xx - 2, pl.ds(0, CROWS), :].astype(F32)
                ).astype(BF16)
                vals = jnp.where(seen, vals.astype(F32), 0.0).astype(BF16)
                ones = jnp.where(seen, 1.0, 0.0).astype(BF16)
            kp[rows, :] = keys
            vp[rows, pl.ds(0, HEAD)] = vals
            vp[rows, pl.ds(HEAD, HEAD)] = ones

    def prepare_pair(s):
        if s == 4:
            prepare(7, (z + 4) % NZ)
        else:
            prepare(2 * s - 1, (z - s + NZ) % NZ)
            prepare(2 * s, (z + s) % NZ)

    def prepare_block():
        for n in range(NZ):
            s = (n + 1) // 2
            zz = z if n == 0 else ((z + s) % NZ if n in (2, 4, 6, 7) else (z - s + NZ) % NZ)
            for xx in range(NX):
                rows = pl.ds(pl.multiple_of(xx * NZ * TOK + zz * TOK, TOK), TOK)
                kb[rows, :] = bb[n, xx, pl.ds(0, TOK), :]
                vb[rows, pl.ds(0, HEAD)] = bb[n, xx, pl.ds(TOK, TOK), :]

    def scores(g, t, keys):
        queries = qbuf[g, pl.ds(t * TILE, TILE), :]
        return lax.dot_general(queries, keys, NT, preferred_element_type=F32) * SCALE

    tiles = range(ROWS // TILE)

    def wide(a, width):
        return jnp.tile(a, (1, width // HEAD))

    def update(g, t, parts, values, initial):
        rows = pl.ds(t * TILE, TILE)
        peak = jnp.max(parts[0], axis=1, keepdims=True)
        for part in parts[1:]:
            peak = jnp.maximum(peak, jnp.max(part, axis=1, keepdims=True))
        high = jnp.broadcast_to(peak, (TILE, HEAD))
        total = None
        if not initial:
            old = top[g, rows, :]
            high = jnp.maximum(old, high)
            total = acc[g, rows, :] * wide(jnp.exp2(old - high), 2 * HEAD)
        for part, ref in zip(parts, values):
            weights = jnp.exp2(part - wide(high, part.shape[1])).astype(BF16)
            product = jnp.dot(weights, ref[...], preferred_element_type=F32)
            total = product if total is None else total + product
        return high, total

    def segment(g, low, up):
        keys = pl.ds(low * CHUNK, (up + 1 - low) * CHUNK)
        raw = [[scores(g, t, kp[keys, :])] for t in tiles]
        for t in tiles:
            rows = pl.ds(t * TILE, TILE)
            high, total = update(g, t, raw[t], [vp.at[keys]], low == 0)
            acc[g, rows, :] = total
            top[g, rows, :] = high

    def last(g):
        far = pl.ds(7 * CHUNK, CHUNK)
        whole = pl.ds(0, g * NZ * TOK)
        diagonal = pl.ds(g * NZ * TOK, NZ * TOK)
        raw = []
        for t in tiles:
            parts = [scores(g, t, kp[far, :])]
            if g:
                parts.append(scores(g, t, kb[whole, :]))
            parts.append(scores(g, t, kb[diagonal, :]) + bias[...])
            raw.append(parts)
        values = [vp.at[far]] + ([vb.at[whole]] if g else []) + [vb.at[diagonal]]
        for t in tiles:
            high, total = update(g, t, raw[t], values, False)
            done = (total[:, :HEAD] / total[:, HEAD:]).astype(BF16)
            for j in range(TILE // TOK):
                h = t * (TILE // TOK) + j
                ost[g, :, pl.ds(h * HEAD, HEAD)] = done[j * TOK : (j + 1) * TOK, :]

    def result_piece(g):
        p = 2 * (x % 2) + c
        return remote(
            ost.at[g],
            out.at[:, pl.ds(pl.multiple_of(p * 1024, 1024), 1024)],
            o_send.at[g],
            o_recv.at[p],
            dev(sec, g, z, x // 2),
        )

    def keep(g):
        return jnp.logical_and(g == x, x // 2 == c)

    def send_result(g):
        @pl.when(keep(g))
        def _():
            p = 2 * (x % 2) + c
            pltpu.make_async_copy(
                ost.at[g], out.at[:, pl.ds(pl.multiple_of(p * 1024, 1024), 1024)], o_recv.at[p]
            ).start()

        @pl.when(jnp.logical_not(keep(g)))
        def _():
            result_piece(g).start()

    row = lax.broadcasted_iota(jnp.int32, (TILE, NZ * TOK), 0) % TOK
    col = lax.broadcasted_iota(jnp.int32, (TILE, NZ * TOK), 1)
    bias[...] = jnp.where(col <= z * TOK + row, 0.0, NEG)
    vb[:, pl.ds(HEAD, HEAD)] = jnp.ones((NX * NZ * TOK, HEAD), BF16)

    groups = [None] * NX

    def step(name):
        op, at = name[0], [int(a) for a in name[1:]]
        if op == "C":
            send_cache()
        elif op == "N":
            send_near()
        elif op == "Q":
            send_queries(at[0])
        elif op == "G":
            sends.pop(("q", at[0])).wait_send()
        elif op == "B":
            send_block()
        elif op == "b":
            begin_block()
        elif op == "o":
            begin_cache()
        elif op == "O":
            arrive(cache_ring, 0)
            prepare(0, z)
        elif op == "c":
            forward(cache_ring, at[0])
        elif op == "k":
            forward(block_ring, at[0])
        elif op == "a":
            arrive(cache_ring, at[0])
            prepare_pair(at[0])
        elif op == "e":
            for s in range(5):
                arrive(block_ring, s)
            prepare_block()
        elif op == "w":
            groups[at[0]] = wait_queries(at[0])
        elif op == "s":
            segment(groups[at[0]], at[1], at[2])
        elif op == "L":
            lax.fori_loop(0, NX, finish, 0)

    def finish(r, carry):
        g = (x + 2 - r + 3 * (r // 2) - 2 * (r // 3)) % NX
        for n in range(NX):
            pl.when(g == n)(functools.partial(last, n))
        send_result(g)
        return carry

    for names in PLAN:
        for name in names.split():
            step(name)

    cache_sent()
    for copy in sends.values():
        copy.wait_send()
    for g in range(NX):

        @pl.when(jnp.logical_not(keep(g)))
        def _():
            result_piece(g).wait_send()

    for p in range(4):
        piece = out.at[:, pl.ds(p * 1024, 1024)]
        remote(piece, piece, o_send.at[p], o_recv.at[p], sibling).wait_recv()


def body(
    q_mant,
    q_scale,
    key_mantissa_block,
    key_exponent_scale,
    value_mantissa_block,
    value_exponent_scale,
    cached_key_rows,
    cached_value_rows,
    start,
):
    vmem = pl.BlockSpec(memory_space=pltpu.VMEM)
    anywhere = pl.BlockSpec(memory_space=pl.ANY)
    dma = pltpu.SemaphoreType.DMA
    result = pl.pallas_call(
        kernel,
        out_shape=pltpu.VMEM((TOK, 4096), BF16),
        in_specs=[
            *[anywhere] * 8,
            pl.BlockSpec(memory_space=pltpu.SMEM),
        ],
        out_specs=vmem,
        scratch_shapes=[
            pltpu.VMEM((TOK, 4096), BF16),
            pltpu.VMEM((TOK, 128), jnp.int32),
            pltpu.VMEM((TOK, 256), BF16),
            pltpu.VMEM((8, TOK), jnp.int32),
            pltpu.VMEM((TOK, 256), BF16),
            pltpu.VMEM((8, TOK), jnp.int32),
            pltpu.VMEM((2, 2 * CROWS, HEAD), BF16),
            pltpu.VMEM((4, ROWS, HEAD), BF16),
            pltpu.VMEM((2, 2 * TOK, HEAD), BF16),
            pltpu.VMEM((NX, ROWS, HEAD), BF16),
            pltpu.VMEM((NZ, NX, 2 * CROWS, HEAD), BF16),
            pltpu.VMEM((NZ, NX, 2 * TOK, HEAD), BF16),
            pltpu.VMEM((NZ * NX * CROWS, HEAD), BF16),
            pltpu.VMEM((NZ * NX * CROWS, 2 * HEAD), BF16),
            pltpu.VMEM((NZ * NX * TOK, HEAD), BF16),
            pltpu.VMEM((NZ * NX * TOK, 2 * HEAD), BF16),
            pltpu.VMEM((NX, ROWS, 2 * HEAD), F32),
            pltpu.VMEM((NX, ROWS, HEAD), F32),
            pltpu.VMEM((TILE, NZ * TOK), F32),
            pltpu.VMEM((NX, TOK, 1024), BF16),
            dma((10,)),
        ]
        + [dma((2,))] * 2
        + [dma((2, 2))] * 2
        + [dma((2,))] * 2
        + [dma((4,))] * 4
        + [dma((5, 2))] * 8,
        compiler_params=pltpu.CompilerParams(
            collective_id=0, has_side_effects=True, vmem_limit_bytes=56 << 20
        ),
        name="attend",
    )(
        q_mant[0],
        q_scale[0],
        key_mantissa_block[0],
        jnp.swapaxes(key_exponent_scale[0], 0, 1),
        value_mantissa_block[0],
        jnp.swapaxes(value_exponent_scale[0], 0, 1),
        cached_key_rows[0],
        cached_value_rows[0],
        start,
    )
    return result[None]


def solution(mesh):
    return jax.shard_map(
        body,
        mesh=mesh,
        in_specs=(
            P("section", "seq", "tensor"),
            P("section", "seq", "tensor"),
            P("section", "seq", "tensor"),
            P("section", "seq", "tensor"),
            P("section", "seq", "tensor"),
            P("section", "seq", "tensor"),
            P("section", "tensor", "seq", None),
            P("section", "tensor", "seq", None),
            P("section"),
        ),
        out_specs=P("section", "seq", "tensor"),
        check_vma=False,
    )
```

```python
import functools
import math

import jax
import jax.numpy as jnp
from jax import lax
from jax.experimental import pallas as pl
from jax.experimental.pallas import tpu as pltpu
from jax.sharding import PartitionSpec as P

BF16, F32 = jnp.bfloat16, jnp.float32
MESH = pl.DeviceIdType.MESH
NX, NZ = 4, 8
HEAD = 128
GROUP_HEADS = 8
TOK = 64
CROWS = 128
ROWS = GROUP_HEADS * TOK
TILE = 128
CHUNK = NX * CROWS
SCALE = (1.0 / math.sqrt(HEAD)) * math.log2(math.e)
NEG = -1e30
PLAN = (
    *("N B C Q0", "Q1 c1 Q2 b", "Q3 o O", "a1 c2 k1", "w0 s002", "w1 s102", "a2 s034 c3 k2"),
    *("s134 w2 s204", "a3 k3", "s056 w3 s306", "s156 s256", "c4 k4", "e a4 L"),
)
NT = (((1,), (1,)), ((), ()))
TN = (((0,), (0,)), ((), ()))


def spread(first, blocks, features):
    row = lax.broadcasted_iota(jnp.int32, (blocks, features), 0)
    col = lax.broadcasted_iota(jnp.int32, (blocks, features), 1)
    return jnp.where(row == first + col // 32, 1.0, 0.0).astype(BF16)


def kernel(
    q_hbm,
    qs_hbm,
    km_hbm,
    ks_hbm,
    vm_hbm,
    vs_hbm,
    ck_hbm,
    cv_hbm,
    start,
    out,
    q_in,
    q_scale,
    k_mant,
    k_scale,
    v_mant,
    v_scale,
    stage,
    qst,
    bst,
    qbuf,
    cb,
    bb,
    kp,
    vp,
    kb,
    vb,
    acc,
    top,
    bias,
    ost,
    load_sem,
    c_send,
    c_recv,
    n_send,
    n_recv,
    b_send,
    b_recv,
    q_send,
    q_recv,
    o_send,
    o_recv,
    rc_send,
    rc_recv,
    sc_send,
    sc_recv,
    rb_send,
    rb_recv,
    sb_send,
    sb_recv,
):
    sec = lax.axis_index("section")
    seq = lax.axis_index("seq")
    ten = lax.axis_index("tensor")
    x, z = seq // NZ, seq % NZ
    yl, c = ten // 2, ten % 2
    other = 1 - sec

    def dev(s, xx, zz, cc):
        return {"section": s, "seq": xx * NZ + zz, "tensor": yl * 2 + cc}

    loads = []
    for i in range(2):
        loads.append((ck_hbm.at[i], stage.at[i, pl.ds(0, CROWS)]))
        loads.append((cv_hbm.at[i], stage.at[i, pl.ds(CROWS, CROWS)]))
    loads += [(q_hbm, q_in), (qs_hbm, q_scale), (km_hbm, k_mant), (ks_hbm, k_scale)]
    loads += [(vm_hbm, v_mant), (vs_hbm, v_scale)]
    loads = [pltpu.make_async_copy(a, b, load_sem.at[n]) for n, (a, b) in enumerate(loads)]
    for cp in loads:
        cp.start()

    def decode():
        power = jnp.exp2(q_scale[...].astype(F32))
        pick = spread(0, 32, 1024)
        for k in range(NX):
            factor = jnp.dot(
                power[:, k * 32 : (k + 1) * 32].astype(BF16), pick, preferred_element_type=F32
            )
            mant = q_in[:, pl.ds(k * 1024, 1024)].astype(F32)
            decoded = (mant * factor).astype(BF16)
            for h in range(GROUP_HEADS):
                qst[k, pl.ds(h * TOK, TOK), :] = decoded[:, h * HEAD : (h + 1) * HEAD]
        pick = spread(0, 8, 256)
        for at, mant, scale in ((0, k_mant, k_scale), (TOK, v_mant, v_scale)):
            power = jnp.exp2(scale[...].astype(F32)).astype(BF16)
            factor = lax.dot_general(power, pick, TN, preferred_element_type=F32)
            decoded = (mant[...].astype(F32) * factor).astype(BF16)
            for i in range(2):
                bst[i, pl.ds(at, TOK), :] = decoded[:, i * HEAD : (i + 1) * HEAD]

    barrier = pltpu.get_barrier_semaphore()
    for ds in range(2):
        for dx in range(NX):
            for dc in range(2):
                if ds == 0 and dx == 0 and dc == 0:
                    continue
                pl.semaphore_signal(
                    barrier,
                    inc=1,
                    device_id=dev((sec + ds) % 2, (x + dx) % NX, z, (c + dc) % 2),
                    device_id_type=MESH,
                )
    for dz in (1, NZ - 1):
        zz = (z + dz) % NZ
        for xx, cc in ((x, c), (x, 1 - c), (2 * c, x // 2), (2 * c + 1, x // 2)):
            pl.semaphore_signal(
                barrier, inc=1, device_id=dev(sec, xx, zz, cc), device_id_type=MESH
            )
    for cp in loads:
        cp.wait()
    decode()
    pl.semaphore_wait(barrier, 23)

    sibling = dev(sec, x, z, 1 - c)

    def remote(src, dst, ssem, rsem, to):
        return pltpu.make_async_remote_copy(
            src_ref=src, dst_ref=dst, send_sem=ssem, recv_sem=rsem, device_id=to, device_id_type=MESH
        )

    sends, recvs = {}, {}

    def launch(key, copy):
        copy.start()
        sends[key] = copy
        recvs[key] = copy

    def received(key):
        recvs.pop(key).wait_recv()

    def cache_piece(i):
        return remote(
            stage.at[i], cb.at[0, x], c_send.at[i], c_recv.at[x % 2], dev(sec, 2 * c + i, z, x // 2)
        )

    def send_cache():
        for i in range(2):

            @pl.when(2 * c + i == x)
            def _():
                pltpu.make_async_copy(stage.at[i], cb.at[0, x], c_recv.at[x % 2]).start()

            @pl.when(2 * c + i != x)
            def _():
                cache_piece(i).start()

            here = cb.at[0, 2 * c + i]
            recvs["c", i] = remote(here, here, c_send.at[i], c_recv.at[i], sibling)

    def cache_sent():
        for i in range(2):

            @pl.when(2 * c + i != x)
            def _():
                cache_piece(i).wait_send()

    def send_near():
        for d in range(2):
            zz = (z + (1, NZ - 1)[d]) % NZ
            for i in range(2):
                sends["n", d, i] = remote(
                    stage.at[i],
                    cb.at[1 + d, x],
                    n_send.at[d, i],
                    n_recv.at[d, x % 2],
                    dev(sec, 2 * c + i, zz, x // 2),
                )
                sends["n", d, i].start()
                here = cb.at[1 + d, 2 * c + i]
                recvs["n", d, i] = remote(here, here, n_send.at[d, i], n_recv.at[d, i], sibling)

    def query_piece(r):
        k = (x + r) % NX
        return remote(
            qst.at[k], qbuf.at[x], q_send.at[r], q_recv.at[x], dev(other, 2 * c + k // 2, z, k % 2)
        )

    def send_queries(r):
        sends["q", r] = query_piece(r)
        sends["q", r].start()
        g = (2 * (x % 2) + c - r + NX) % NX
        recvs["q", r] = remote(qbuf.at[g], qbuf.at[g], q_send.at[r], q_recv.at[g], sibling)

    def wait_queries(r):
        received(("q", r))
        return (2 * (x % 2) + c - r + NX) % NX


    def send_block():
        for i in range(2):
            sends["b", i] = remote(
                bst.at[i], bb.at[0, x], b_send.at[i], b_recv.at[x % 2], dev(other, 2 * c + i, z, x // 2)
            )
            sends["b", i].start()
            here = bb.at[0, 2 * c + i]
            recvs["b", i] = remote(here, here, b_send.at[i], b_recv.at[i], sibling)

    onward = (dev(sec, x, (z + 1) % NZ, c), dev(sec, x, (z + NZ - 1) % NZ, c))

    def slot(s, d):
        return 0 if s == 0 else (7 if s == 4 else 2 * s - 1 + d)

    def unit(buf, n, s, d, core):
        return buf.at[n, pl.ds(2 * core + d, 1) if s == 4 else pl.ds(2 * core, 2)]

    def hop(ring, s, d):
        buf, rs, rr = ring[:3]
        src, dst = unit(buf, slot(s - 1, d), s, d, c), unit(buf, slot(s, d), s, d, c)
        return remote(src, dst, rs.at[s, d], rr.at[s, d], onward[d])

    def across(ring, s, d):
        here = unit(ring[0], slot(s, d), s, d, c)
        if s == 4:
            to = dev(sec, x, (z + (1, NZ - 1)[d]) % NZ, 1 - c)
            return remote(
                unit(ring[0], slot(3, d), 4, d, c), here, ring[3].at[s, d], ring[4].at[s, d], to
            )
        return remote(here, here, ring[3].at[s, d], ring[4].at[s, d], sibling)

    def from_sibling(ring, s, d):
        here = unit(ring[0], slot(s, d), s, d, 1 - c)
        return remote(here, here, ring[3].at[s, d], ring[4].at[s, d], sibling)

    cache_ring = (cb, rc_send, rc_recv, sc_send, sc_recv)
    block_ring = (bb, rb_send, rb_recv, sb_send, sb_recv)

    def hops(ring, s):
        for d in range(2):
            launch(("hop", id(ring), s, d), hop(ring, s, d))

    def share(ring, s, d):
        copy = across(ring, s, d)
        copy.start()
        sends["across", id(ring), s, d] = copy
        recvs["across", id(ring), s, d] = from_sibling(ring, s, d)

    def begin_block():
        for i in range(2):
            received(("b", i))
        hops(block_ring, 1)
        share(block_ring, 0, 0)

    def begin_cache():
        for i in range(2):
            received(("c", i))
        share(cache_ring, 0, 0)

    def forward(ring, s):
        for d in range(2):
            if s == 1 and ring is cache_ring:
                for n in range(2):
                    received(("n", d, n))
            else:
                received(("hop", id(ring), s, d))
            if s < 4:
                launch(("hop", id(ring), s + 1, d), hop(ring, s + 1, d))
        if s < 4:
            for d in range(2):
                share(ring, s, d)
        if s == 3:
            for d in range(2):
                share(ring, 4, d)

    def arrive(ring, s):
        for d in range(2 if s else 1):
            received(("across", id(ring), s, d))

    limit = start[0]

    def prepare(n, zz):
        for xx in range(NX):
            rows = pl.ds(n * NX * CROWS + xx * CROWS, CROWS)
            keys = cb[n, xx, pl.ds(0, CROWS), :]
            vals = cb[n, xx, pl.ds(CROWS, CROWS), :]
            ones = jnp.ones((CROWS, HEAD), BF16)
            if xx >= 2:
                at = xx * NZ * CROWS + zz * CROWS
                seen = at + lax.broadcasted_iota(jnp.int32, (CROWS, HEAD), 0) < limit
                keys = jnp.where(
                    seen, keys.astype(F32), cb[n, xx - 2, pl.ds(0, CROWS), :].astype(F32)
                ).astype(BF16)
                vals = jnp.where(seen, vals.astype(F32), 0.0).astype(BF16)
                ones = jnp.where(seen, 1.0, 0.0).astype(BF16)
            kp[rows, :] = keys
            vp[rows, pl.ds(0, HEAD)] = vals
            vp[rows, pl.ds(HEAD, HEAD)] = ones

    def prepare_pair(s):
        if s == 4:
            prepare(7, (z + 4) % NZ)
        else:
            prepare(2 * s - 1, (z - s + NZ) % NZ)
            prepare(2 * s, (z + s) % NZ)

    def prepare_block():
        for n in range(NZ):
            s = (n + 1) // 2
            zz = z if n == 0 else ((z + s) % NZ if n in (2, 4, 6, 7) else (z - s + NZ) % NZ)
            for xx in range(NX):
                rows = pl.ds(pl.multiple_of(xx * NZ * TOK + zz * TOK, TOK), TOK)
                kb[rows, :] = bb[n, xx, pl.ds(0, TOK), :]
                vb[rows, pl.ds(0, HEAD)] = bb[n, xx, pl.ds(TOK, TOK), :]

    def scores(g, t, keys):
        queries = qbuf[g, pl.ds(t * TILE, TILE), :]
        return lax.dot_general(queries, keys, NT, preferred_element_type=F32) * SCALE

    tiles = range(ROWS // TILE)

    def wide(a, width):
        return jnp.tile(a, (1, width // HEAD))

    def update(g, t, parts, values, initial):
        rows = pl.ds(t * TILE, TILE)
        peak = jnp.max(parts[0], axis=1, keepdims=True)
        for part in parts[1:]:
            peak = jnp.maximum(peak, jnp.max(part, axis=1, keepdims=True))
        high = jnp.broadcast_to(peak, (TILE, HEAD))
        total = None
        if not initial:
            old = top[g, rows, :]
            high = jnp.maximum(old, high)
            total = acc[g, rows, :] * wide(jnp.exp2(old - high), 2 * HEAD)
        for part, ref in zip(parts, values):
            weights = jnp.exp2(part - wide(high, part.shape[1])).astype(BF16)
            product = jnp.dot(weights, ref[...], preferred_element_type=F32)
            total = product if total is None else total + product
        return high, total

    def segment(g, low, up):
        keys = pl.ds(low * CHUNK, (up + 1 - low) * CHUNK)
        raw = [[scores(g, t, kp[keys, :])] for t in tiles]
        for t in tiles:
            rows = pl.ds(t * TILE, TILE)
            high, total = update(g, t, raw[t], [vp.at[keys]], low == 0)
            acc[g, rows, :] = total
            top[g, rows, :] = high

    def last(g):
        far = pl.ds(7 * CHUNK, CHUNK)
        whole = pl.ds(0, g * NZ * TOK)
        diagonal = pl.ds(g * NZ * TOK, NZ * TOK)
        raw = []
        for t in tiles:
            parts = [scores(g, t, kp[far, :])]
            if g:
                parts.append(scores(g, t, kb[whole, :]))
            parts.append(scores(g, t, kb[diagonal, :]) + bias[...])
            raw.append(parts)
        values = [vp.at[far]] + ([vb.at[whole]] if g else []) + [vb.at[diagonal]]
        for t in tiles:
            high, total = update(g, t, raw[t], values, False)
            done = (total[:, :HEAD] / total[:, HEAD:]).astype(BF16)
            for j in range(TILE // TOK):
                h = t * (TILE // TOK) + j
                ost[g, :, pl.ds(h * HEAD, HEAD)] = done[j * TOK : (j + 1) * TOK, :]

    def result_piece(g):
        p = 2 * (x % 2) + c
        return remote(
            ost.at[g],
            out.at[:, pl.ds(pl.multiple_of(p * 1024, 1024), 1024)],
            o_send.at[g],
            o_recv.at[p],
            dev(sec, g, z, x // 2),
        )

    def keep(g):
        return jnp.logical_and(g == x, x // 2 == c)

    def send_result(g):
        @pl.when(keep(g))
        def _():
            p = 2 * (x % 2) + c
            pltpu.make_async_copy(
                ost.at[g], out.at[:, pl.ds(pl.multiple_of(p * 1024, 1024), 1024)], o_recv.at[p]
            ).start()

        @pl.when(jnp.logical_not(keep(g)))
        def _():
            result_piece(g).start()

    row = lax.broadcasted_iota(jnp.int32, (TILE, NZ * TOK), 0) % TOK
    col = lax.broadcasted_iota(jnp.int32, (TILE, NZ * TOK), 1)
    bias[...] = jnp.where(col <= z * TOK + row, 0.0, NEG)
    vb[:, pl.ds(HEAD, HEAD)] = jnp.ones((NX * NZ * TOK, HEAD), BF16)

    groups = [None] * NX

    def step(name):
        op, at = name[0], [int(a) for a in name[1:]]
        if op == "C":
            send_cache()
        elif op == "N":
            send_near()
        elif op == "Q":
            send_queries(at[0])
        elif op == "G":
            sends.pop(("q", at[0])).wait_send()
        elif op == "B":
            send_block()
        elif op == "b":
            begin_block()
        elif op == "o":
            begin_cache()
        elif op == "O":
            arrive(cache_ring, 0)
            prepare(0, z)
        elif op == "c":
            forward(cache_ring, at[0])
        elif op == "k":
            forward(block_ring, at[0])
        elif op == "a":
            arrive(cache_ring, at[0])
            prepare_pair(at[0])
        elif op == "e":
            for s in range(5):
                arrive(block_ring, s)
            prepare_block()
        elif op == "w":
            groups[at[0]] = wait_queries(at[0])
        elif op == "s":
            segment(groups[at[0]], at[1], at[2])
        elif op == "L":
            lax.fori_loop(0, NX, finish, 0)

    def finish(r, carry):
        g = (x + 2 - r + 3 * (r // 2) - 2 * (r // 3)) % NX
        for n in range(NX):
            pl.when(g == n)(functools.partial(last, n))
        send_result(g)
        return carry

    for names in PLAN:
        for name in names.split():
            step(name)

    cache_sent()
    for copy in sends.values():
        copy.wait_send()
    for g in range(NX):

        @pl.when(jnp.logical_not(keep(g)))
        def _():
            result_piece(g).wait_send()

    for p in range(4):
        piece = out.at[:, pl.ds(p * 1024, 1024)]
        remote(piece, piece, o_send.at[p], o_recv.at[p], sibling).wait_recv()


def body(
    q_mant,
    q_scale,
    key_mantissa_block,
    key_exponent_scale,
    value_mantissa_block,
    value_exponent_scale,
    cached_key_rows,
    cached_value_rows,
    start,
):
    vmem = pl.BlockSpec(memory_space=pltpu.VMEM)
    anywhere = pl.BlockSpec(memory_space=pl.ANY)
    dma = pltpu.SemaphoreType.DMA
    result = pl.pallas_call(
        kernel,
        out_shape=pltpu.VMEM((TOK, 4096), BF16),
        in_specs=[
            *[anywhere] * 8,
            pl.BlockSpec(memory_space=pltpu.SMEM),
        ],
        out_specs=vmem,
        scratch_shapes=[
            pltpu.VMEM((TOK, 4096), BF16),
            pltpu.VMEM((TOK, 128), jnp.int32),
            pltpu.VMEM((TOK, 256), BF16),
            pltpu.VMEM((8, TOK), jnp.int32),
            pltpu.VMEM((TOK, 256), BF16),
            pltpu.VMEM((8, TOK), jnp.int32),
            pltpu.VMEM((2, 2 * CROWS, HEAD), BF16),
            pltpu.VMEM((4, ROWS, HEAD), BF16),
            pltpu.VMEM((2, 2 * TOK, HEAD), BF16),
            pltpu.VMEM((NX, ROWS, HEAD), BF16),
            pltpu.VMEM((NZ, NX, 2 * CROWS, HEAD), BF16),
            pltpu.VMEM((NZ, NX, 2 * TOK, HEAD), BF16),
            pltpu.VMEM((NZ * NX * CROWS, HEAD), BF16),
            pltpu.VMEM((NZ * NX * CROWS, 2 * HEAD), BF16),
            pltpu.VMEM((NZ * NX * TOK, HEAD), BF16),
            pltpu.VMEM((NZ * NX * TOK, 2 * HEAD), BF16),
            pltpu.VMEM((NX, ROWS, 2 * HEAD), F32),
            pltpu.VMEM((NX, ROWS, HEAD), F32),
            pltpu.VMEM((TILE, NZ * TOK), F32),
            pltpu.VMEM((NX, TOK, 1024), BF16),
            dma((10,)),
        ]
        + [dma((2,))] * 2
        + [dma((2, 2))] * 2
        + [dma((2,))] * 2
        + [dma((4,))] * 4
        + [dma((5, 2))] * 8,
        compiler_params=pltpu.CompilerParams(
            collective_id=0, has_side_effects=True, vmem_limit_bytes=56 << 20
        ),
        name="attend",
    )(
        q_mant[0],
        q_scale[0],
        key_mantissa_block[0],
        jnp.swapaxes(key_exponent_scale[0], 0, 1),
        value_mantissa_block[0],
        jnp.swapaxes(value_exponent_scale[0], 0, 1),
        cached_key_rows[0],
        cached_value_rows[0],
        start,
    )
    return result[None]


def solution(mesh):
    return jax.shard_map(
        body,
        mesh=mesh,
        in_specs=(
            P("section", "seq", "tensor"),
            P("section", "seq", "tensor"),
            P("section", "seq", "tensor"),
            P("section", "seq", "tensor"),
            P("section", "seq", "tensor"),
            P("section", "seq", "tensor"),
            P("section", "tensor", "seq", None),
            P("section", "tensor", "seq", None),
            P("section"),
        ),
        out_specs=P("section", "seq", "tensor"),
        check_vma=False,
    )
```

```python
import functools
import math

import jax
import jax.numpy as jnp
from jax import lax
from jax.experimental import pallas as pl
from jax.experimental.pallas import tpu as pltpu
from jax.sharding import PartitionSpec as P

BF16, F32 = jnp.bfloat16, jnp.float32
MESH = pl.DeviceIdType.MESH
NX, NZ = 4, 8
HEAD = 128
GROUP_HEADS = 8
TOK = 64
CROWS = 128
ROWS = GROUP_HEADS * TOK
TILE = 128
CHUNK = NX * CROWS
SCALE = (1.0 / math.sqrt(HEAD)) * math.log2(math.e)
NEG = -1e30
PLAN = (
    *("N B C Q0", "Q1 c1 Q2 b", "Q3 o O", "a1 c2 k1", "w0 s002", "w1 s102", "a2 s034 c3 k2"),
    *("s134 w2 s204", "a3 k3", "s056 w3 s306", "c4 k4", "e a4 L"),
)
NT = (((1,), (1,)), ((), ()))
TN = (((0,), (0,)), ((), ()))


def spread(first, blocks, features):
    row = lax.broadcasted_iota(jnp.int32, (blocks, features), 0)
    col = lax.broadcasted_iota(jnp.int32, (blocks, features), 1)
    return jnp.where(row == first + col // 32, 1.0, 0.0).astype(BF16)


def kernel(
    q_hbm,
    qs_hbm,
    km_hbm,
    ks_hbm,
    vm_hbm,
    vs_hbm,
    ck_hbm,
    cv_hbm,
    start,
    out,
    q_in,
    q_scale,
    k_mant,
    k_scale,
    v_mant,
    v_scale,
    stage,
    qst,
    bst,
    qbuf,
    cb,
    bb,
    kp,
    vp,
    kb,
    vb,
    acc,
    top,
    bias,
    ost,
    load_sem,
    c_send,
    c_recv,
    n_send,
    n_recv,
    b_send,
    b_recv,
    q_send,
    q_recv,
    o_send,
    o_recv,
    rc_send,
    rc_recv,
    sc_send,
    sc_recv,
    rb_send,
    rb_recv,
    sb_send,
    sb_recv,
):
    sec = lax.axis_index("section")
    seq = lax.axis_index("seq")
    ten = lax.axis_index("tensor")
    x, z = seq // NZ, seq % NZ
    yl, c = ten // 2, ten % 2
    other = 1 - sec

    def dev(s, xx, zz, cc):
        return {"section": s, "seq": xx * NZ + zz, "tensor": yl * 2 + cc}

    loads = []
    for i in range(2):
        loads.append((ck_hbm.at[i], stage.at[i, pl.ds(0, CROWS)]))
        loads.append((cv_hbm.at[i], stage.at[i, pl.ds(CROWS, CROWS)]))
    loads += [(q_hbm, q_in), (qs_hbm, q_scale), (km_hbm, k_mant), (ks_hbm, k_scale)]
    loads += [(vm_hbm, v_mant), (vs_hbm, v_scale)]
    loads = [pltpu.make_async_copy(a, b, load_sem.at[n]) for n, (a, b) in enumerate(loads)]
    for cp in loads:
        cp.start()

    def decode():
        power = jnp.exp2(q_scale[...].astype(F32))
        pick = spread(0, 32, 1024)
        for k in range(NX):
            factor = jnp.dot(
                power[:, k * 32 : (k + 1) * 32].astype(BF16), pick, preferred_element_type=F32
            )
            mant = q_in[:, pl.ds(k * 1024, 1024)].astype(F32)
            decoded = (mant * factor).astype(BF16)
            for h in range(GROUP_HEADS):
                qst[k, pl.ds(h * TOK, TOK), :] = decoded[:, h * HEAD : (h + 1) * HEAD]
        pick = spread(0, 8, 256)
        for at, mant, scale in ((0, k_mant, k_scale), (TOK, v_mant, v_scale)):
            power = jnp.exp2(scale[...].astype(F32)).astype(BF16)
            factor = lax.dot_general(power, pick, TN, preferred_element_type=F32)
            decoded = (mant[...].astype(F32) * factor).astype(BF16)
            for i in range(2):
                bst[i, pl.ds(at, TOK), :] = decoded[:, i * HEAD : (i + 1) * HEAD]

    barrier = pltpu.get_barrier_semaphore()
    for ds in range(2):
        for dx in range(NX):
            for dc in range(2):
                if ds == 0 and dx == 0 and dc == 0:
                    continue
                pl.semaphore_signal(
                    barrier,
                    inc=1,
                    device_id=dev((sec + ds) % 2, (x + dx) % NX, z, (c + dc) % 2),
                    device_id_type=MESH,
                )
    for dz in (1, NZ - 1):
        zz = (z + dz) % NZ
        for xx, cc in ((x, c), (x, 1 - c), (2 * c, x // 2), (2 * c + 1, x // 2)):
            pl.semaphore_signal(
                barrier, inc=1, device_id=dev(sec, xx, zz, cc), device_id_type=MESH
            )
    for cp in loads:
        cp.wait()
    decode()
    pl.semaphore_wait(barrier, 23)

    sibling = dev(sec, x, z, 1 - c)

    def remote(src, dst, ssem, rsem, to):
        return pltpu.make_async_remote_copy(
            src_ref=src, dst_ref=dst, send_sem=ssem, recv_sem=rsem, device_id=to, device_id_type=MESH
        )

    sends, recvs = {}, {}

    def launch(key, copy):
        copy.start()
        sends[key] = copy
        recvs[key] = copy

    def received(key):
        recvs.pop(key).wait_recv()

    def cache_piece(i):
        return remote(
            stage.at[i], cb.at[0, x], c_send.at[i], c_recv.at[x % 2], dev(sec, 2 * c + i, z, x // 2)
        )

    def send_cache():
        for i in range(2):

            @pl.when(2 * c + i == x)
            def _():
                pltpu.make_async_copy(stage.at[i], cb.at[0, x], c_recv.at[x % 2]).start()

            @pl.when(2 * c + i != x)
            def _():
                cache_piece(i).start()

            here = cb.at[0, 2 * c + i]
            recvs["c", i] = remote(here, here, c_send.at[i], c_recv.at[i], sibling)

    def cache_sent():
        for i in range(2):

            @pl.when(2 * c + i != x)
            def _():
                cache_piece(i).wait_send()

    def send_near():
        for d in range(2):
            zz = (z + (1, NZ - 1)[d]) % NZ
            for i in range(2):
                sends["n", d, i] = remote(
                    stage.at[i],
                    cb.at[1 + d, x],
                    n_send.at[d, i],
                    n_recv.at[d, x % 2],
                    dev(sec, 2 * c + i, zz, x // 2),
                )
                sends["n", d, i].start()
                here = cb.at[1 + d, 2 * c + i]
                recvs["n", d, i] = remote(here, here, n_send.at[d, i], n_recv.at[d, i], sibling)

    def query_piece(r):
        k = (x + r) % NX
        return remote(
            qst.at[k], qbuf.at[x], q_send.at[r], q_recv.at[x], dev(other, 2 * c + k // 2, z, k % 2)
        )

    def send_queries(r):
        sends["q", r] = query_piece(r)
        sends["q", r].start()
        g = (2 * (x % 2) + c - r + NX) % NX
        recvs["q", r] = remote(qbuf.at[g], qbuf.at[g], q_send.at[r], q_recv.at[g], sibling)

    def wait_queries(r):
        received(("q", r))
        return (2 * (x % 2) + c - r + NX) % NX


    def send_block():
        for i in range(2):
            sends["b", i] = remote(
                bst.at[i], bb.at[0, x], b_send.at[i], b_recv.at[x % 2], dev(other, 2 * c + i, z, x // 2)
            )
            sends["b", i].start()
            here = bb.at[0, 2 * c + i]
            recvs["b", i] = remote(here, here, b_send.at[i], b_recv.at[i], sibling)

    onward = (dev(sec, x, (z + 1) % NZ, c), dev(sec, x, (z + NZ - 1) % NZ, c))

    def slot(s, d):
        return 0 if s == 0 else (7 if s == 4 else 2 * s - 1 + d)

    def unit(buf, n, s, d, core):
        return buf.at[n, pl.ds(2 * core + d, 1) if s == 4 else pl.ds(2 * core, 2)]

    def hop(ring, s, d):
        buf, rs, rr = ring[:3]
        src, dst = unit(buf, slot(s - 1, d), s, d, c), unit(buf, slot(s, d), s, d, c)
        return remote(src, dst, rs.at[s, d], rr.at[s, d], onward[d])

    def across(ring, s, d):
        here = unit(ring[0], slot(s, d), s, d, c)
        if s == 4:
            to = dev(sec, x, (z + (1, NZ - 1)[d]) % NZ, 1 - c)
            return remote(
                unit(ring[0], slot(3, d), 4, d, c), here, ring[3].at[s, d], ring[4].at[s, d], to
            )
        return remote(here, here, ring[3].at[s, d], ring[4].at[s, d], sibling)

    def from_sibling(ring, s, d):
        here = unit(ring[0], slot(s, d), s, d, 1 - c)
        return remote(here, here, ring[3].at[s, d], ring[4].at[s, d], sibling)

    cache_ring = (cb, rc_send, rc_recv, sc_send, sc_recv)
    block_ring = (bb, rb_send, rb_recv, sb_send, sb_recv)

    def hops(ring, s):
        for d in range(2):
            launch(("hop", id(ring), s, d), hop(ring, s, d))

    def share(ring, s, d):
        copy = across(ring, s, d)
        copy.start()
        sends["across", id(ring), s, d] = copy
        recvs["across", id(ring), s, d] = from_sibling(ring, s, d)

    def begin_block():
        for i in range(2):
            received(("b", i))
        hops(block_ring, 1)
        share(block_ring, 0, 0)

    def begin_cache():
        for i in range(2):
            received(("c", i))
        share(cache_ring, 0, 0)

    def forward(ring, s):
        for d in range(2):
            if s == 1 and ring is cache_ring:
                for n in range(2):
                    received(("n", d, n))
            else:
                received(("hop", id(ring), s, d))
            if s < 4:
                launch(("hop", id(ring), s + 1, d), hop(ring, s + 1, d))
        if s < 4:
            for d in range(2):
                share(ring, s, d)
        if s == 3:
            for d in range(2):
                share(ring, 4, d)

    def arrive(ring, s):
        for d in range(2 if s else 1):
            received(("across", id(ring), s, d))

    limit = start[0]

    def prepare(n, zz):
        for xx in range(NX):
            rows = pl.ds(n * NX * CROWS + xx * CROWS, CROWS)
            keys = cb[n, xx, pl.ds(0, CROWS), :]
            vals = cb[n, xx, pl.ds(CROWS, CROWS), :]
            ones = jnp.ones((CROWS, HEAD), BF16)
            if xx >= 2:
                at = xx * NZ * CROWS + zz * CROWS
                seen = at + lax.broadcasted_iota(jnp.int32, (CROWS, HEAD), 0) < limit
                keys = jnp.where(
                    seen, keys.astype(F32), cb[n, xx - 2, pl.ds(0, CROWS), :].astype(F32)
                ).astype(BF16)
                vals = jnp.where(seen, vals.astype(F32), 0.0).astype(BF16)
                ones = jnp.where(seen, 1.0, 0.0).astype(BF16)
            kp[rows, :] = keys
            vp[rows, pl.ds(0, HEAD)] = vals
            vp[rows, pl.ds(HEAD, HEAD)] = ones

    def prepare_pair(s):
        if s == 4:
            prepare(7, (z + 4) % NZ)
        else:
            prepare(2 * s - 1, (z - s + NZ) % NZ)
            prepare(2 * s, (z + s) % NZ)

    def prepare_block():
        for n in range(NZ):
            s = (n + 1) // 2
            zz = z if n == 0 else ((z + s) % NZ if n in (2, 4, 6, 7) else (z - s + NZ) % NZ)
            for xx in range(NX):
                rows = pl.ds(pl.multiple_of(xx * NZ * TOK + zz * TOK, TOK), TOK)
                kb[rows, :] = bb[n, xx, pl.ds(0, TOK), :]
                vb[rows, pl.ds(0, HEAD)] = bb[n, xx, pl.ds(TOK, TOK), :]

    def scores(g, t, keys):
        queries = qbuf[g, pl.ds(t * TILE, TILE), :]
        return lax.dot_general(queries, keys, NT, preferred_element_type=F32) * SCALE

    tiles = range(ROWS // TILE)

    def wide(a, width):
        return jnp.tile(a, (1, width // HEAD))

    def update(g, t, parts, values, initial):
        rows = pl.ds(t * TILE, TILE)
        peak = jnp.max(parts[0], axis=1, keepdims=True)
        for part in parts[1:]:
            peak = jnp.maximum(peak, jnp.max(part, axis=1, keepdims=True))
        high = jnp.broadcast_to(peak, (TILE, HEAD))
        total = None
        if not initial:
            old = top[g, rows, :]
            high = jnp.maximum(old, high)
            total = acc[g, rows, :] * wide(jnp.exp2(old - high), 2 * HEAD)
        for part, ref in zip(parts, values):
            weights = jnp.exp2(part - wide(high, part.shape[1])).astype(BF16)
            product = jnp.dot(weights, ref[...], preferred_element_type=F32)
            total = product if total is None else total + product
        return high, total

    def segment(g, low, up):
        keys = pl.ds(low * CHUNK, (up + 1 - low) * CHUNK)
        raw = [[scores(g, t, kp[keys, :])] for t in tiles]
        for t in tiles:
            rows = pl.ds(t * TILE, TILE)
            high, total = update(g, t, raw[t], [vp.at[keys]], low == 0)
            acc[g, rows, :] = total
            top[g, rows, :] = high

    def last(g):
        far = pl.ds(7 * CHUNK, CHUNK)
        whole = pl.ds(0, g * NZ * TOK)
        diagonal = pl.ds(g * NZ * TOK, NZ * TOK)
        raw = []
        for t in tiles:
            parts = [scores(g, t, kp[far, :])]
            if g:
                parts.append(scores(g, t, kb[whole, :]))
            parts.append(scores(g, t, kb[diagonal, :]) + bias[...])
            raw.append(parts)
        values = [vp.at[far]] + ([vb.at[whole]] if g else []) + [vb.at[diagonal]]
        for t in tiles:
            high, total = update(g, t, raw[t], values, False)
            done = (total[:, :HEAD] / total[:, HEAD:]).astype(BF16)
            for j in range(TILE // TOK):
                h = t * (TILE // TOK) + j
                ost[g, :, pl.ds(h * HEAD, HEAD)] = done[j * TOK : (j + 1) * TOK, :]

    def result_piece(g):
        p = 2 * (x % 2) + c
        return remote(
            ost.at[g],
            out.at[:, pl.ds(pl.multiple_of(p * 1024, 1024), 1024)],
            o_send.at[g],
            o_recv.at[p],
            dev(sec, g, z, x // 2),
        )

    def keep(g):
        return jnp.logical_and(g == x, x // 2 == c)

    def send_result(g):
        @pl.when(keep(g))
        def _():
            p = 2 * (x % 2) + c
            pltpu.make_async_copy(
                ost.at[g], out.at[:, pl.ds(pl.multiple_of(p * 1024, 1024), 1024)], o_recv.at[p]
            ).start()

        @pl.when(jnp.logical_not(keep(g)))
        def _():
            result_piece(g).start()

    row = lax.broadcasted_iota(jnp.int32, (TILE, NZ * TOK), 0) % TOK
    col = lax.broadcasted_iota(jnp.int32, (TILE, NZ * TOK), 1)
    bias[...] = jnp.where(col <= z * TOK + row, 0.0, NEG)
    vb[:, pl.ds(HEAD, HEAD)] = jnp.ones((NX * NZ * TOK, HEAD), BF16)

    groups = [None] * NX

    def step(name):
        op, at = name[0], [int(a) for a in name[1:]]
        if op == "C":
            send_cache()
        elif op == "N":
            send_near()
        elif op == "Q":
            send_queries(at[0])
        elif op == "G":
            sends.pop(("q", at[0])).wait_send()
        elif op == "B":
            send_block()
        elif op == "b":
            begin_block()
        elif op == "o":
            begin_cache()
        elif op == "O":
            arrive(cache_ring, 0)
            prepare(0, z)
        elif op == "c":
            forward(cache_ring, at[0])
        elif op == "k":
            forward(block_ring, at[0])
        elif op == "a":
            arrive(cache_ring, at[0])
            prepare_pair(at[0])
        elif op == "e":
            for s in range(5):
                arrive(block_ring, s)
            prepare_block()
        elif op == "w":
            groups[at[0]] = wait_queries(at[0])
        elif op == "s":
            segment(groups[at[0]], at[1], at[2])
        elif op == "L":
            lax.fori_loop(0, NX, finish, 0)

    def finish(r, carry):
        g = (2 * (x % 2) + c - r + NX) % NX

        @pl.when(r % 3 != 0)
        def _():
            segment(g, 5, 6)

        for n in range(NX):
            pl.when(g == n)(functools.partial(last, n))
        send_result(g)
        return carry

    for names in PLAN:
        for name in names.split():
            step(name)

    cache_sent()
    for copy in sends.values():
        copy.wait_send()
    for g in range(NX):

        @pl.when(jnp.logical_not(keep(g)))
        def _():
            result_piece(g).wait_send()

    for p in range(4):
        piece = out.at[:, pl.ds(p * 1024, 1024)]
        remote(piece, piece, o_send.at[p], o_recv.at[p], sibling).wait_recv()


def body(
    q_mant,
    q_scale,
    key_mantissa_block,
    key_exponent_scale,
    value_mantissa_block,
    value_exponent_scale,
    cached_key_rows,
    cached_value_rows,
    start,
):
    vmem = pl.BlockSpec(memory_space=pltpu.VMEM)
    anywhere = pl.BlockSpec(memory_space=pl.ANY)
    dma = pltpu.SemaphoreType.DMA
    result = pl.pallas_call(
        kernel,
        out_shape=pltpu.VMEM((TOK, 4096), BF16),
        in_specs=[
            *[anywhere] * 8,
            pl.BlockSpec(memory_space=pltpu.SMEM),
        ],
        out_specs=vmem,
        scratch_shapes=[
            pltpu.VMEM((TOK, 4096), BF16),
            pltpu.VMEM((TOK, 128), jnp.int32),
            pltpu.VMEM((TOK, 256), BF16),
            pltpu.VMEM((8, TOK), jnp.int32),
            pltpu.VMEM((TOK, 256), BF16),
            pltpu.VMEM((8, TOK), jnp.int32),
            pltpu.VMEM((2, 2 * CROWS, HEAD), BF16),
            pltpu.VMEM((4, ROWS, HEAD), BF16),
            pltpu.VMEM((2, 2 * TOK, HEAD), BF16),
            pltpu.VMEM((NX, ROWS, HEAD), BF16),
            pltpu.VMEM((NZ, NX, 2 * CROWS, HEAD), BF16),
            pltpu.VMEM((NZ, NX, 2 * TOK, HEAD), BF16),
            pltpu.VMEM((NZ * NX * CROWS, HEAD), BF16),
            pltpu.VMEM((NZ * NX * CROWS, 2 * HEAD), BF16),
            pltpu.VMEM((NZ * NX * TOK, HEAD), BF16),
            pltpu.VMEM((NZ * NX * TOK, 2 * HEAD), BF16),
            pltpu.VMEM((NX, ROWS, 2 * HEAD), F32),
            pltpu.VMEM((NX, ROWS, HEAD), F32),
            pltpu.VMEM((TILE, NZ * TOK), F32),
            pltpu.VMEM((NX, TOK, 1024), BF16),
            dma((10,)),
        ]
        + [dma((2,))] * 2
        + [dma((2, 2))] * 2
        + [dma((2,))] * 2
        + [dma((4,))] * 4
        + [dma((5, 2))] * 8,
        compiler_params=pltpu.CompilerParams(
            collective_id=0, has_side_effects=True, vmem_limit_bytes=56 << 20
        ),
        name="attend",
    )(
        q_mant[0],
        q_scale[0],
        key_mantissa_block[0],
        jnp.swapaxes(key_exponent_scale[0], 0, 1),
        value_mantissa_block[0],
        jnp.swapaxes(value_exponent_scale[0], 0, 1),
        cached_key_rows[0],
        cached_value_rows[0],
        start,
    )
    return result[None]


def solution(mesh):
    return jax.shard_map(
        body,
        mesh=mesh,
        in_specs=(
            P("section", "seq", "tensor"),
            P("section", "seq", "tensor"),
            P("section", "seq", "tensor"),
            P("section", "seq", "tensor"),
            P("section", "seq", "tensor"),
            P("section", "seq", "tensor"),
            P("section", "tensor", "seq", None),
            P("section", "tensor", "seq", None),
            P("section"),
        ),
        out_specs=P("section", "seq", "tensor"),
        check_vma=False,
    )
```
